128 devices in a mesh: section: 2 (over z_lo), patch: 4 (over y), shard: 16 (over z_hi, x, core).
Axes of the slice: x: 4, y: 4, z: 4 (z_hi: 2, z_lo: 2; z = z_hi * 2 + z_lo), core: 2. Of those that a mesh axis runs over, the one named last changes fastest.
Arguments:
- hidden: bfloat16 [32, 1024, 2432], P('shard', 'patch'), may hold values from -6 to 6
- text_kv: bfloat16 [2, 32, 154, 2432], P('section', 'shard'), may hold values from -6 to 6, as said below
- stale_kv: bfloat16 [2, 32, 1024, 2432], P('section', 'shard', 'patch'), may hold values from -6 to 6, as said below
- modulation: float32 [2, 32, 3, 2432], P('section', 'shard'), may hold values from -3 to 3
- score_gain: float32 [2, 64], P('section'), may hold values from 1.5 to 4
- qkv_weight: bfloat16 [2, 2432, 3648], P('section', 'shard'), may hold values from -0.125 to 0.125
- out_weight: bfloat16 [2, 1216, 2432], P('section', None, 'shard'), may hold values from -0.15625 to 0.15625
- final_mod: float32 [32, 2, 2432], P('shard'), may hold values from -3 to 3
- final_weight: bfloat16 [2432, 64], replicated, may hold values from -0.125 to 0.125
- latent: float32 [32, 1024, 64], P('shard', ('patch', 'section')), may hold values from -6 to 6
- step_index: int32 [32], P('shard'), may hold values from 0 to 27
Outputs:
- new_kv: bfloat16 [2, 32, 1024, 2432], P('section', 'shard', 'patch')
- latent_next: float32 [32, 1024, 64], P('shard', ('patch', 'section'))
- denoised: float32 [32, 1024, 64], P('shard', ('patch', 'section'))
The draws below stay inside these ranges and needn't reach their ends.
Inputs may be any that keep to these rules, and one draw needn't show every extreme that they name: `text_kv`: in every row the first 1216 columns are 19 heads of 64 key features, each head with mean square one up to bfloat16 rounding. `stale_kv`: in every row the first 1216 columns are 19 heads of 64 key features, each head with mean square one up to bfloat16 rounding.
All inputs are finite; a program needn't handle non-finite values.
Results may differ from the reference program's by a relative error of at most 0.008.
Values may be sent and summed in bfloat16 or wider, within the bound.
No kernel may reach another device: no remote copies, remote signals or barrier semaphores. Data moves between devices by JAX's collectives and lax.ppermute only.
A program may use at most 192 MiB of HBM per device.

```python
import math
import jax
import jax.numpy as jnp
from jax import lax

D = 2432
HEADS = 19
HEAD = 64
IMG = 1024
TXT = 154
CH = 64
NSTEPS = 28
HW = 1216
QKV = 3648
IMG_DEV = 256
REQ = 32
LAYERS = 2
N_PATCH = 4


def keys_values(key, rows, salt):
    key = jax.random.fold_in(key, salt)
    key_angle, key_value = jax.random.split(key, 2)
    half = HEAD // 2
    angle = jax.random.uniform(key_angle, (LAYERS, REQ, rows, HEADS, half), jnp.float32, -math.pi, math.pi)
    keys = jnp.concatenate([jnp.cos(angle), jnp.sin(angle)], -1) * math.sqrt(2.0)
    keys = keys.reshape(LAYERS, REQ, rows, HW)
    values = jnp.clip(jax.random.normal(key_value, (LAYERS, REQ, rows, HW), jnp.float32), -6.0, 6.0)
    return jnp.concatenate([keys, values], -1).astype(jnp.bfloat16)


def draw_text_kv(key, part):
    return keys_values(key, TXT, 101)


def draw_stale_kv(key, part):
    return keys_values(key, IMG, 202)


def plant(array, stream_key, least, top_value):
    longest = array.shape.index(max(array.shape))
    spots = []
    for shift in (0, 1):
        where = [jax.random.randint(jax.random.fold_in(stream_key, axis), (), 0, length) for axis, length in enumerate(array.shape)]
        where[longest] = (where[longest] + shift) % array.shape[longest]
        spots.append(tuple(where))
    return array.at[spots[0]].set(least).at[spots[1]].set(top_value)


def shard_levels(own_key, shape, shards, least, high):
    factor_of = 1.0
    for dim, parts in shards:
        heights = jax.random.uniform(jax.random.fold_in(jax.random.fold_in(own_key, 6), dim), (parts,), jnp.float32, least / len(shards), high / len(shards))
        factor_of = factor_of * jnp.repeat(jnp.exp(heights), shape[dim] // parts).reshape((-1,) + (1,) * (len(shape) - 1 - dim))
    return factor_of


def gaussian(own_key, shape, spread, reach, cuts=(), held_as=jnp.bfloat16):
    array = jax.random.normal(own_key, shape, jnp.float32) * spread
    if len(cuts) > 0:
        array = shard_levels(own_key, shape, cuts, -0.22, 0.18) * array
    return jnp.clip(array, min=-reach, max=reach).astype(held_as)


def setup_inputs(seed: int = 0) -> dict:
    seeds = jax.random.split(jax.random.key(seed), 12)
    return {
        "hidden": gaussian(seeds[0], (REQ, IMG, D), 1.0, 6.0, ((0, 16), (1, 4))),
        "text_kv": draw_text_kv(jax.random.fold_in(seeds[11], 71), 0),
        "stale_kv": draw_stale_kv(jax.random.fold_in(seeds[11], 71), 0),
        "modulation": gaussian(seeds[3], (LAYERS, REQ, 3, D), 0.6, 3.0, ((0, 2), (1, 16)), jnp.float32),
        "score_gain": jnp.clip(jnp.exp(math.log(4.0) - 0.98082925 * jax.random.uniform(seeds[4], (LAYERS, HEAD), jnp.float32) ** shard_levels(seeds[4], (LAYERS, HEAD), ((0, 2),), -0.2, 0.2)), 1.5, 4.0),
        "qkv_weight": gaussian(seeds[5], (LAYERS, D, QKV), D ** -0.5, 0.125, ((0, 2), (1, 16))),
        "out_weight": gaussian(seeds[6], (LAYERS, HW, D), HW ** -0.5, 0.15625, ((0, 2), (2, 16))),
        "final_mod": gaussian(seeds[7], (REQ, 2, D), 0.5, 3.0, ((0, 16),), jnp.float32),
        "final_weight": gaussian(seeds[8], (D, CH), D ** -0.5, 0.125),
        "latent": gaussian(seeds[9], (REQ, IMG, CH), 1.0, 6.0, ((0, 16), (1, 8)), jnp.float32),
        "step_index": plant(jax.random.randint(seeds[10], (REQ,), 0, NSTEPS), jax.random.fold_in(seeds[10], 1), 0, NSTEPS - 1).astype(jnp.int32),
    }


eps_norm = 1e-06
flow_shift = 3.0

def sigma_of(step):
    s = 1.0 - step.astype(jnp.float32) / NSTEPS
    return flow_shift * s / (1.0 + (flow_shift - 1.0) * s)

def modulated(xf, shift, scale):
    mean = lax.optimization_barrier(jnp.mean(xf, -1, keepdims=True))
    cent = xf - mean
    var = lax.optimization_barrier(jnp.mean(cent * cent, -1, keepdims=True))
    return cent * lax.rsqrt(var + eps_norm) * (1.0 + scale) + shift

def attend(query, keys_all):
    count = keys_all.shape[0]
    keys = keys_all[:, :HW].reshape(count, HEADS, HEAD).astype(jnp.float32)
    values = keys_all[:, HW:].reshape(count, HEADS, HEAD).astype(jnp.float32)
    scores = jnp.einsum('qhe,khe->hqk', query.astype(jnp.float32), keys)
    expo = jnp.exp(scores)
    total = lax.optimization_barrier(jnp.sum(expo, -1))
    weights = expo.astype(jnp.bfloat16)
    mixed = jnp.einsum('hqk,khe->qhe', weights.astype(jnp.float32), values)
    mixed = mixed / jnp.transpose(total)[:, :, None]
    return mixed.reshape(query.shape[0], HW).astype(jnp.bfloat16)

def reference(hidden, text_kv, stale_kv, modulation, score_gain, qkv_weight, out_weight, final_mod, final_weight, latent, step_index):

    def one_request(items):
        x, text_r, stale_r, mod_r, fmod, lat, step = items
        fresh_list = []
        for layer in range(LAYERS):
            xf = x.astype(jnp.float32)
            normed = modulated(xf, mod_r[layer, 0], mod_r[layer, 1]).astype(jnp.bfloat16)
            proj_in = jnp.dot(normed, qkv_weight[layer], preferred_element_type=jnp.float32)
            q = proj_in[:, :HW].reshape(IMG, HEADS, HEAD)
            k = proj_in[:, HW:2 * HW].reshape(IMG, HEADS, HEAD)
            v = proj_in[:, 2 * HW:]
            q_hat = q * lax.rsqrt(lax.optimization_barrier(jnp.mean(q * q, -1, keepdims=True)) + eps_norm)
            k_hat = k * lax.rsqrt(lax.optimization_barrier(jnp.mean(k * k, -1, keepdims=True)) + eps_norm)
            fresh = jnp.concatenate([k_hat.reshape(IMG, HW).astype(jnp.bfloat16), v.astype(jnp.bfloat16)], -1)
            query = (q_hat * score_gain[layer] / math.sqrt(HEAD)).astype(jnp.bfloat16)
            pieces = []
            for patch in range(N_PATCH):
                low = patch * IMG_DEV
                high = low + IMG_DEV
                mixed = jnp.concatenate([stale_r[layer, :low], fresh[low:high], stale_r[layer, high:]], 0)
                keys_all = jnp.concatenate([text_r[layer], mixed], 0)
                pieces.append(attend(query[low:high], keys_all))
            attn = jnp.concatenate(pieces, 0)
            proj = jnp.dot(attn, out_weight[layer], preferred_element_type=jnp.float32)
            x = (xf + mod_r[layer, 2] * proj).astype(jnp.bfloat16)
            fresh_list.append(fresh)
        final = modulated(x.astype(jnp.float32), fmod[0], fmod[1]).astype(jnp.bfloat16)
        velocity = jnp.dot(final, final_weight, preferred_element_type=jnp.float32)
        sig = sigma_of(step)
        sig_next = sigma_of(step + 1)
        return (jnp.stack(fresh_list), lat + (sig_next - sig) * velocity, lat - sig * velocity)
    fresh_all, latent_next, denoised = lax.map(one_request, (hidden, jnp.transpose(text_kv, (1, 0, 2, 3)), jnp.transpose(stale_kv, (1, 0, 2, 3)), jnp.transpose(modulation, (1, 0, 2, 3)), final_mod, latent, step_index))
    return (jnp.transpose(fresh_all, (1, 0, 2, 3)), latent_next, denoised)
```

```python
import math

import jax
import jax.numpy as jnp
from jax import lax
from jax.experimental import pallas as pl
from jax.experimental.pallas import tpu as pltpu
from jax.sharding import PartitionSpec as P

HEAD = 64
NSTEPS = 28
D = 2432
HW = 1216
ROWS = 256
TXT = 154
TXT_PAD = 160
KEYS = 4 * ROWS + TXT_PAD
BLK = 304
ZC = 1280
XC = D - ZC
LANE = 128
NT = 256

eps_norm = 1e-06
flow_shift = 3.0


def sigma_of(step):
    s = 1.0 - step.astype(jnp.float32) / NSTEPS
    return flow_shift * s / (1.0 + (flow_shift - 1.0) * s)


def shard_pairs(flip_z=0, dx=0, flip_core=0):
    pairs = []
    for z in range(2):
        for x in range(4):
            for c in range(2):
                src = z * 8 + x * 2 + c
                dst = (z ^ flip_z) * 8 + ((x + dx) % 4) * 2 + (c ^ flip_core)
                pairs.append((src, dst))
    return pairs


def ring_pairs(step):
    return [(i, (i + step) % 4) for i in range(4)]


def x_shift(value, dx):
    return lax.ppermute(value, "shard", shard_pairs(dx=dx))


def z_flip(value):
    return lax.ppermute(value, "shard", shard_pairs(flip_z=1))


def core_flip(value):
    return lax.ppermute(value, "shard", shard_pairs(flip_core=1))


def y_shift(value, dy):
    return lax.ppermute(value, "patch", ring_pairs(dy))


def ring_gather(value, shift):
    half = value.shape[0] // 2
    before = shift(value, 1)
    after = shift(value, -1)
    far_low = shift(before[:half], 1)
    far_high = shift(after[half:], -1)
    return before, after, far_low, far_high


def group_scale(p, ones_ref):
    sq = p * p
    hi = sq.astype(jnp.bfloat16)
    lo = (sq - hi.astype(jnp.float32)).astype(jnp.bfloat16)
    ones = ones_ref[...]
    total = jnp.dot(hi, ones, preferred_element_type=jnp.float32) + jnp.dot(
        lo, ones, preferred_element_type=jnp.float32
    )
    return lax.rsqrt(total * (1.0 / HEAD) + eps_norm)


def norm_rows(src_ref, shift_ref, scale_ref, dst_ref):
    step = 32

    def body(i, _):
        r = pl.multiple_of(i * step, step)
        xf = src_ref[pl.ds(r, step), :].astype(jnp.float32)
        mean = jnp.mean(xf, -1, keepdims=True)
        cent = xf - mean
        var = jnp.mean(cent * cent, -1, keepdims=True)
        out = cent * lax.rsqrt(var + eps_norm) * (1.0 + scale_ref[...]) + shift_ref[...]
        dst_ref[pl.ds(r, step), :] = out.astype(jnp.bfloat16)
        return 0

    lax.fori_loop(0, ROWS // step, body, 0)


def layer_kernel(final, *refs):
    (sc, x_ref, mod_ref, fmod_ref, gain_ref, fw_ref) = refs[:6]
    mine = refs[6:13]
    theirs = refs[13:20]
    (st_b, st_a, st_l, st_h, text_ref) = refs[20:25]
    if final:
        vel_ref, fresh_ref = refs[25:27]
        scratch = refs[27:]
        (w_kv, w_q, w_o, kv, normed, qbuf, attn, ones, sems, x_out) = scratch
    else:
        x_out, fresh_ref = refs[25:27]
        scratch = refs[27:]
        (w_kv, w_q, w_o, kv, normed, qbuf, attn, ones, sems) = scratch
    row_of = lambda slot, j: pl.multiple_of(sc[1 + slot * 4 + j], 16)

    def spread_z(pieces, cols, dst, dst_cols, sem):
        zs, zb, za, zl, zh = pieces[:5]
        for j, ref in enumerate((zs, zb, za)):
            for slot in range(2):
                pltpu.make_async_copy(
                    ref.at[pl.ds(slot * BLK, BLK), cols],
                    dst.at[pl.ds(row_of(slot, j), BLK), dst_cols],
                    sem,
                ).start()
        for slot, ref in enumerate((zl, zh)):
            pltpu.make_async_copy(
                ref.at[:, cols], dst.at[pl.ds(row_of(slot, 3), BLK), dst_cols], sem
            ).start()

    def spread_x(pieces, dst, dst_cols, sem):
        for slot in range(2):
            for j in range(4):
                pltpu.make_async_copy(
                    pieces[5 + slot].at[pl.ds(j * BLK, BLK), :],
                    dst.at[pl.ds(row_of(slot, j), BLK), dst_cols],
                    sem,
                ).start()

    def fetch(kv_pieces, oq_pieces):
        spread_z(kv_pieces, pl.ds(0, ZC), w_kv, pl.ds(0, ZC), sems.at[0])
        spread_x(kv_pieces, w_kv, pl.ds(ZC, XC), sems.at[1])
        spread_z(oq_pieces, pl.ds(ZC - LANE, LANE), w_q, pl.ds(0, LANE), sems.at[2])
        spread_x(oq_pieces, w_q, pl.ds(LANE, XC), sems.at[2])

    def fetch_out(oq_pieces):
        spread_z(oq_pieces, pl.ds(0, ZC), w_o, pl.ds(0, ZC), sems.at[4])

    @pl.when(sc[0] == 0)
    def _():
        fetch(mine, theirs)

    @pl.when(sc[0] != 0)
    def _():
        fetch(theirs, mine)

    row = ROWS
    for ref, count in ((st_b, ROWS), (st_a, ROWS), (st_l, ROWS // 2), (st_h, ROWS // 2), (text_ref, TXT_PAD)):
        pltpu.make_async_copy(ref, kv.at[pl.ds(row, count), :], sems.at[3]).start()
        row += count

    @pl.when(sc[0] == 0)
    def _():
        fetch_out(theirs)

    @pl.when(sc[0] != 0)
    def _():
        fetch_out(mine)

    def wait(dst, sem):
        pltpu.make_async_copy(dst, dst, sem).wait()

    norm_rows(x_ref, mod_ref.at[0:1, :], mod_ref.at[1:2, :], normed)
    gi = lax.broadcasted_iota(jnp.int32, (NT, NT), 0) // HEAD
    gj = lax.broadcasted_iota(jnp.int32, (NT, NT), 1) // HEAD
    ones[...] = jnp.where(gi == gj, 1.0, 0.0).astype(jnp.bfloat16)

    wait(w_kv.at[:, pl.ds(0, ZC)], sems.at[0])

    def key_block(j, _):
        c = pl.multiple_of(j * NT, NT)
        p = jnp.dot(normed[...], w_kv[:, pl.ds(c, NT)], preferred_element_type=jnp.float32)
        col = lax.broadcasted_iota(jnp.int32, (ROWS, NT), 1) + c
        out = (p * jnp.where(col < HW, group_scale(p, ones), 1.0)).astype(jnp.bfloat16)
        kv[pl.ds(0, ROWS), pl.ds(c, NT)] = out
        fresh_ref[:, pl.ds(c, NT)] = out
        return 0

    lax.fori_loop(0, ZC // NT, key_block, 0)
    wait(w_kv.at[:, pl.ds(ZC, XC)], sems.at[1])
    vw = 384

    def value_block(j, _):
        c = pl.multiple_of(ZC + j * vw, LANE)
        p = jnp.dot(normed[...], w_kv[:, pl.ds(c, vw)], preferred_element_type=jnp.float32)
        out = p.astype(jnp.bfloat16)
        kv[pl.ds(0, ROWS), pl.ds(c, vw)] = out
        fresh_ref[:, pl.ds(c, vw)] = out
        return 0

    lax.fori_loop(0, XC // vw, value_block, 0)
    wait(w_q, sems.at[2])

    def query_block(j, _):
        c = pl.multiple_of(j * NT, NT)
        p = jnp.dot(normed[...], w_q[:, pl.ds(c, NT)], preferred_element_type=jnp.float32)
        qbuf[:, pl.ds(c, NT)] = p * group_scale(p, ones) * gain_ref[:, pl.ds(c, NT)]
        return 0

    lax.fori_loop(0, ZC // NT, query_block, 0)
    wait(kv.at[pl.ds(ROWS, KEYS - ROWS), :], sems.at[3])

    low = lax.broadcasted_iota(jnp.int32, (ROWS, LANE), 1) < HEAD
    chunks = [(i * ROWS, ROWS) for i in range(4)] + [(4 * ROWS, TXT_PAD)]
    contract = (((1,), (1,)), ((), ()))
    one_rows = jnp.ones((ROWS, LANE), jnp.bfloat16)
    text_rows = jnp.where(
        lax.broadcasted_iota(jnp.int32, (TXT_PAD, LANE), 0) < TXT, 1.0, 0.0
    ).astype(jnp.bfloat16)

    def one_head(q, kc, vc):
        acc = None
        for start, count in chunks:
            k = kv[pl.ds(start, count), pl.ds(kc, LANE)]
            v = kv[pl.ds(start, count), pl.ds(vc, LANE)]
            s = lax.dot_general(q, k, contract, preferred_element_type=jnp.float32)
            w = jnp.exp(s).astype(jnp.bfloat16)
            v_one = jnp.concatenate([v, one_rows if count == ROWS else text_rows], 1)
            part = jnp.dot(w, v_one, preferred_element_type=jnp.float32)
            acc = part if acc is None else acc + part
        return acc[:, :LANE], acc[:, LANE:]

    def pair(i, _):
        c = pl.multiple_of(i * LANE, LANE)
        n = pl.multiple_of(c + LANE, LANE)
        mixed = jnp.where(low, qbuf[:, pl.ds(n, LANE)], qbuf[:, pl.ds(c, LANE)])
        q2 = pltpu.roll(mixed, HEAD, 1)
        q_even = jnp.where(low, q2, 0.0).astype(jnp.bfloat16)
        q_odd = jnp.where(low, 0.0, q2).astype(jnp.bfloat16)
        vc = pl.multiple_of(c + 9 * LANE, LANE)
        vn = pl.multiple_of(c + 10 * LANE, LANE)
        a_even, t_even = one_head(q_even, c, vc)
        a_odd, t_odd = one_head(q_odd, c, vn)
        out = jnp.where(low, a_odd, a_even) / jnp.where(low, t_odd, t_even)
        attn[:, pl.ds(c, LANE)] = pltpu.roll(out, HEAD, 1).astype(jnp.bfloat16)
        return 0

    lax.fori_loop(0, 9, pair, 0)
    q2 = pltpu.roll(qbuf[:, pl.ds(9 * LANE, LANE)], HEAD, 1)
    a_last, t_last = one_head(jnp.where(low, q2, 0.0).astype(jnp.bfloat16), 9 * LANE, 18 * LANE)
    out = jnp.where(low, 0.0, a_last / t_last)
    attn[:, pl.ds(9 * LANE, LANE)] = pltpu.roll(out, HEAD, 1).astype(jnp.bfloat16)

    wait(w_o, sems.at[4])

    def out_block(c, width):
        proj = lax.dot_general(
            attn[...], w_o[pl.ds(c, width), :], contract, preferred_element_type=jnp.float32
        )
        xf = x_ref[:, pl.ds(c, width)].astype(jnp.float32)
        gate = mod_ref[2:3, pl.ds(c, width)]
        x_out[:, pl.ds(c, width)] = (xf + gate * proj).astype(jnp.bfloat16)

    def out_body(j, _):
        out_block(pl.multiple_of(j * NT, NT), NT)
        return 0

    lax.fori_loop(0, D // NT, out_body, 0)
    out_block((D // NT) * NT, D % NT)
    if final:
        norm_rows(x_out, fmod_ref.at[0:1, :], fmod_ref.at[1:2, :], normed)
        vel_ref[...] = jnp.dot(normed[...], fw_ref[...], preferred_element_type=jnp.float32)


def run_layer(scalars, x, mod, fmod, gain, fw, mine, theirs, stale, text, final):
    vmem = pl.BlockSpec(memory_space=pltpu.VMEM)
    hbm = pl.BlockSpec(memory_space=pl.ANY)
    first = (
        jax.ShapeDtypeStruct((ROWS, fw.shape[1]), jnp.float32)
        if final
        else jax.ShapeDtypeStruct((ROWS, D), jnp.bfloat16)
    )
    scratch = [
        pltpu.VMEM((D, D), jnp.bfloat16),
        pltpu.VMEM((D, ZC), jnp.bfloat16),
        pltpu.VMEM((D, ZC), jnp.bfloat16),
        pltpu.VMEM((KEYS, D), jnp.bfloat16),
        pltpu.VMEM((ROWS, D), jnp.bfloat16),
        pltpu.VMEM((ROWS, ZC), jnp.float32),
        pltpu.VMEM((ROWS, ZC), jnp.bfloat16),
        pltpu.VMEM((NT, NT), jnp.bfloat16),
        pltpu.SemaphoreType.DMA((5,)),
    ]
    if final:
        scratch.append(pltpu.VMEM((ROWS, D), jnp.bfloat16))
    return pl.pallas_call(
        lambda *refs: layer_kernel(final, *refs),
        name="last_layer" if final else "first_layer",
        out_shape=(first, jax.ShapeDtypeStruct((ROWS, D), jnp.bfloat16)),
        in_specs=[pl.BlockSpec(memory_space=pltpu.SMEM)] + [vmem] * 5 + [hbm] * 19,
        out_specs=(vmem, vmem),
        scratch_shapes=scratch,
        compiler_params=pltpu.CompilerParams(vmem_limit_bytes=56 << 20),
    )(scalars, x, mod, fmod, gain, fw, *mine, *theirs, *stale, text)


def on_device(
    hidden,
    text_kv,
    stale_kv,
    modulation,
    score_gain,
    qkv_weight,
    out_weight,
    final_mod,
    final_weight,
    latent,
    step_index,
):
    section = lax.axis_index("section")
    shard = lax.axis_index("shard")
    z_hi, x_at, core = shard // 8, (shard // 2) % 4, shard % 2

    qkv = qkv_weight[0]
    half_kv = qkv[:, HW:]
    half_oq = jnp.concatenate([out_weight[0].T, qkv[:, :HW]], 1)
    keep = jnp.where(core == 0, half_kv, half_oq)
    give = jnp.where(core == 0, half_oq, half_kv)
    got = core_flip(give)
    block = jnp.concatenate(
        [jnp.where(core == 0, keep, got), jnp.where(core == 0, got, keep)], 0
    )
    block_z, block_x = block[:, :ZC], block[:, ZC:]
    pair_z = jnp.concatenate([block_z, z_flip(block_z)], 0)
    four_x = jnp.concatenate([block_x, *ring_gather(block_x, x_shift)], 0)
    mine = (pair_z, *ring_gather(pair_z, x_shift), four_x, z_flip(four_x))
    theirs = tuple(core_flip(piece) for piece in mine)

    stale = [ring_gather(stale_kv[0, r], y_shift) for r in range(2)]
    text = jnp.pad(text_kv[0], ((0, 0), (0, TXT_PAD - TXT), (0, 0)))
    gain = jnp.tile(score_gain[0] * (1.0 / math.sqrt(HEAD)), ZC // HEAD)[None, :]
    rows = [
        ((z_hi ^ slot) * 4 + (x_at + dx) % 4) * BLK for slot in range(2) for dx in (0, 3, 1, 2)
    ]
    scalars = jnp.stack([core, *rows]).astype(jnp.int32)

    def layer(x, r, final):
        return run_layer(
            scalars, x, modulation[0, r], final_mod[r], gain, final_weight,
            mine, theirs, stale[r], text[r], final,
        )

    fresh_first, arrived = [], []
    for r in range(2):
        x_next, fresh = layer(hidden[r], r, False)
        fresh_first.append(fresh)
        arrived.append(lax.ppermute(x_next, "section", [(0, 1)]))
    fresh_out, velocity = [], []
    for r in range(2):
        vel, fresh = layer(arrived[r], r, True)
        velocity.append(vel)
        fresh_out.append(jnp.where(section == 0, fresh_first[r], fresh))
    velocity = jnp.stack(velocity)
    half = latent.shape[1]
    sent = lax.ppermute(velocity[:, :half].astype(jnp.bfloat16), "section", [(1, 0)])
    velocity_mine = jnp.where(section == 0, sent.astype(jnp.float32), velocity[:, half:])
    sig = sigma_of(step_index)[:, None, None]
    sig_next = sigma_of(step_index + 1)[:, None, None]
    latent_next = latent + (sig_next - sig) * velocity_mine
    denoised = latent - sig * velocity_mine
    return (jnp.stack(fresh_out)[None], latent_next, denoised)


def solution(mesh):
    in_specs = (
        P("shard", "patch", None),
        P("section", "shard", None, None),
        P("section", "shard", "patch", None),
        P("section", "shard", None, None),
        P("section", None),
        P("section", "shard", None),
        P("section", None, "shard"),
        P("shard", None, None),
        P(),
        P("shard", ("patch", "section"), None),
        P("shard"),
    )
    out_specs = (
        P("section", "shard", "patch", None),
        P("shard", ("patch", "section"), None),
        P("shard", ("patch", "section"), None),
    )
    return jax.shard_map(
        on_device, mesh=mesh, in_specs=in_specs, out_specs=out_specs, check_vma=False
    )
```

```python
import math

import jax
import jax.numpy as jnp
from jax import lax
from jax.experimental import pallas as pl
from jax.experimental.pallas import tpu as pltpu
from jax.sharding import PartitionSpec as P

HEAD = 64
NSTEPS = 28
D = 2432
HW = 1216
ROWS = 256
TXT = 154
TXT_PAD = 160
KEYS = 4 * ROWS + TXT_PAD
BLK = 304
ZC = 1280
XC = D - ZC
LANE = 128
NT = 256

eps_norm = 1e-06
flow_shift = 3.0


def sigma_of(step):
    s = 1.0 - step.astype(jnp.float32) / NSTEPS
    return flow_shift * s / (1.0 + (flow_shift - 1.0) * s)


def shard_pairs(flip_z=0, dx=0, flip_core=0):
    pairs = []
    for z in range(2):
        for x in range(4):
            for c in range(2):
                src = z * 8 + x * 2 + c
                dst = (z ^ flip_z) * 8 + ((x + dx) % 4) * 2 + (c ^ flip_core)
                pairs.append((src, dst))
    return pairs


def ring_pairs(step):
    return [(i, (i + step) % 4) for i in range(4)]


def x_shift(value, dx):
    return lax.ppermute(value, "shard", shard_pairs(dx=dx))


def z_flip(value):
    return lax.ppermute(value, "shard", shard_pairs(flip_z=1))


def core_flip(value):
    return lax.ppermute(value, "shard", shard_pairs(flip_core=1))


def y_shift(value, dy):
    return lax.ppermute(value, "patch", ring_pairs(dy))


def x_relay(value):
    pairs = []
    for z in range(2):
        for x in range(4):
            for c in range(2):
                dx = 1 if c == 0 else -1
                pairs.append((z * 8 + x * 2 + c, z * 8 + ((x + dx) % 4) * 2 + c))
    return lax.ppermute(value, "shard", pairs)


def y_relay(value):
    pairs = []
    for y in range(4):
        for k in range(16):
            dy = 1 if k % 2 == 0 else -1
            pairs.append((y * 16 + k, ((y + dy) % 4) * 16 + k))
    return lax.ppermute(value, ("patch", "shard"), pairs)


def after(value, *earlier):
    return lax.optimization_barrier((value, *earlier))[0]


def group_scale(p, ones_ref):
    sq = p * p
    hi = sq.astype(jnp.bfloat16)
    lo = (sq - hi.astype(jnp.float32)).astype(jnp.bfloat16)
    ones = ones_ref[...]
    total = jnp.dot(hi, ones, preferred_element_type=jnp.float32) + jnp.dot(
        lo, ones, preferred_element_type=jnp.float32
    )
    return lax.rsqrt(total * (1.0 / HEAD) + eps_norm)


def norm_rows(src_ref, shift_ref, scale_ref, dst_ref):
    step = 32

    def body(i, _):
        r = pl.multiple_of(i * step, step)
        xf = src_ref[pl.ds(r, step), :].astype(jnp.float32)
        mean = jnp.mean(xf, -1, keepdims=True)
        cent = xf - mean
        var = jnp.mean(cent * cent, -1, keepdims=True)
        out = cent * lax.rsqrt(var + eps_norm) * (1.0 + scale_ref[...]) + shift_ref[...]
        dst_ref[pl.ds(r, step), :] = out.astype(jnp.bfloat16)
        return 0

    lax.fori_loop(0, ROWS // step, body, 0)


def layer_kernel(final, req, *refs):
    (sc, x_ref, mod_ref, fmod_ref, gain_ref, fw_ref) = refs[:6]
    mod_ref, fmod_ref = mod_ref.at[req], fmod_ref.at[req]
    if not final:
        x_ref = x_ref.at[req]
    mine = refs[6:16]
    theirs = refs[16:26]
    stale = refs[26:29]
    text_ref = refs[29]
    if final:
        vel_ref, fresh_ref = refs[30:32]
        scratch = refs[32:]
        (w_kv, w_q, w_o, kv, normed, qbuf, attn, ones, sems, x_out) = scratch
    else:
        x_out, fresh_ref = refs[30:32]
        scratch = refs[32:]
        (w_kv, w_q, w_o, kv, normed, qbuf, attn, ones, sems) = scratch
    row_of = lambda slot, j: pl.multiple_of(sc[1 + slot * 4 + j], 16)

    def put(ref, at, cols, dst, slot, j, dst_cols, sem):
        pltpu.make_async_copy(
            ref.at[pl.ds(at, BLK), cols], dst.at[pl.ds(row_of(slot, j), BLK), dst_cols], sem
        ).start()

    def spread_z(pieces, cols, dst, dst_cols, sem):
        block, opposite = pieces[:2]
        put(block, 0, cols, dst, 0, 0, dst_cols, sem)
        put(opposite, 0, cols, dst, 1, 0, dst_cols, sem)
        for j, ref in enumerate(pieces[2:5]):
            for slot in range(2):
                put(ref, slot * BLK, cols, dst, slot, j + 1, dst_cols, sem)

    def spread_x(pieces, dst, dst_cols, sem):
        cols = pl.ds(0, XC)
        put(pieces[0], 0, pl.ds(ZC, XC), dst, 0, 0, dst_cols, sem)
        for j, ref in enumerate(pieces[5:8]):
            put(ref, 0, cols, dst, 0, j + 1, dst_cols, sem)
        for j in range(3):
            put(pieces[8], j * BLK, cols, dst, 1, j, dst_cols, sem)
        put(pieces[9], 0, cols, dst, 1, 3, dst_cols, sem)

    def fetch(kv_pieces, oq_pieces):
        spread_z(kv_pieces, pl.ds(0, ZC), w_kv, pl.ds(0, ZC), sems.at[0])
        spread_x(kv_pieces, w_kv, pl.ds(ZC, XC), sems.at[1])
        spread_z(oq_pieces, pl.ds(ZC - LANE, LANE), w_q, pl.ds(0, LANE), sems.at[2])
        spread_x(oq_pieces, w_q, pl.ds(LANE, XC), sems.at[2])

    def fetch_out(oq_pieces):
        spread_z(oq_pieces, pl.ds(0, ZC), w_o, pl.ds(0, ZC), sems.at[4])

    @pl.when(sc[0] == 0)
    def _():
        fetch(mine, theirs)

    @pl.when(sc[0] != 0)
    def _():
        fetch(theirs, mine)

    for j, ref in enumerate((*stale, text_ref)):
        count = ROWS if j < 3 else TXT_PAD
        pltpu.make_async_copy(
            ref.at[req], kv.at[pl.ds((j + 1) * ROWS, count), :], sems.at[3]
        ).start()

    @pl.when(sc[0] == 0)
    def _():
        fetch_out(theirs)

    @pl.when(sc[0] != 0)
    def _():
        fetch_out(mine)

    def wait(dst, sem):
        pltpu.make_async_copy(dst, dst, sem).wait()

    norm_rows(x_ref, mod_ref.at[0:1, :], mod_ref.at[1:2, :], normed)
    gi = lax.broadcasted_iota(jnp.int32, (NT, NT), 0) // HEAD
    gj = lax.broadcasted_iota(jnp.int32, (NT, NT), 1) // HEAD
    ones[...] = jnp.where(gi == gj, 1.0, 0.0).astype(jnp.bfloat16)

    wait(w_kv.at[:, pl.ds(0, ZC)], sems.at[0])

    def key_block(j, _):
        c = pl.multiple_of(j * NT, NT)
        p = jnp.dot(normed[...], w_kv[:, pl.ds(c, NT)], preferred_element_type=jnp.float32)
        col = lax.broadcasted_iota(jnp.int32, (ROWS, NT), 1) + c
        out = (p * jnp.where(col < HW, group_scale(p, ones), 1.0)).astype(jnp.bfloat16)
        kv[pl.ds(0, ROWS), pl.ds(c, NT)] = out
        fresh_ref[:, pl.ds(c, NT)] = out
        return 0

    lax.fori_loop(0, ZC // NT, key_block, 0)
    wait(w_kv.at[:, pl.ds(ZC, XC)], sems.at[1])
    vw = 384

    def value_block(j, _):
        c = pl.multiple_of(ZC + j * vw, LANE)
        p = jnp.dot(normed[...], w_kv[:, pl.ds(c, vw)], preferred_element_type=jnp.float32)
        out = p.astype(jnp.bfloat16)
        kv[pl.ds(0, ROWS), pl.ds(c, vw)] = out
        fresh_ref[:, pl.ds(c, vw)] = out
        return 0

    lax.fori_loop(0, XC // vw, value_block, 0)
    wait(w_q, sems.at[2])

    def query_block(j, _):
        c = pl.multiple_of(j * NT, NT)
        p = jnp.dot(normed[...], w_q[:, pl.ds(c, NT)], preferred_element_type=jnp.float32)
        qbuf[:, pl.ds(c, NT)] = p * group_scale(p, ones) * gain_ref[:, pl.ds(c, NT)]
        return 0

    lax.fori_loop(0, ZC // NT, query_block, 0)
    wait(kv.at[pl.ds(ROWS, KEYS - ROWS), :], sems.at[3])

    low = lax.broadcasted_iota(jnp.int32, (ROWS, LANE), 1) < HEAD
    chunks = [(i * ROWS, ROWS) for i in range(4)] + [(4 * ROWS, TXT_PAD)]
    contract = (((1,), (1,)), ((), ()))
    one_rows = jnp.ones((ROWS, LANE), jnp.bfloat16)
    text_rows = jnp.where(
        lax.broadcasted_iota(jnp.int32, (TXT_PAD, LANE), 0) < TXT, 1.0, 0.0
    ).astype(jnp.bfloat16)

    def one_head(q, kc, vc):
        acc = None
        for start, count in chunks:
            k = kv[pl.ds(start, count), pl.ds(kc, LANE)]
            v = kv[pl.ds(start, count), pl.ds(vc, LANE)]
            s = lax.dot_general(q, k, contract, preferred_element_type=jnp.float32)
            w = jnp.exp(s).astype(jnp.bfloat16)
            v_one = jnp.concatenate([v, one_rows if count == ROWS else text_rows], 1)
            part = jnp.dot(w, v_one, preferred_element_type=jnp.float32)
            acc = part if acc is None else acc + part
        return acc[:, :LANE], acc[:, LANE:]

    def pair(i, _):
        c = pl.multiple_of(i * LANE, LANE)
        n = pl.multiple_of(c + LANE, LANE)
        mixed = jnp.where(low, qbuf[:, pl.ds(n, LANE)], qbuf[:, pl.ds(c, LANE)])
        q2 = pltpu.roll(mixed, HEAD, 1)
        q_even = jnp.where(low, q2, 0.0).astype(jnp.bfloat16)
        q_odd = jnp.where(low, 0.0, q2).astype(jnp.bfloat16)
        vc = pl.multiple_of(c + 9 * LANE, LANE)
        vn = pl.multiple_of(c + 10 * LANE, LANE)
        a_even, t_even = one_head(q_even, c, vc)
        a_odd, t_odd = one_head(q_odd, c, vn)
        out = jnp.where(low, a_odd, a_even) / jnp.where(low, t_odd, t_even)
        attn[:, pl.ds(c, LANE)] = pltpu.roll(out, HEAD, 1).astype(jnp.bfloat16)
        return 0

    lax.fori_loop(0, 9, pair, 0)
    q2 = pltpu.roll(qbuf[:, pl.ds(9 * LANE, LANE)], HEAD, 1)
    a_last, t_last = one_head(jnp.where(low, q2, 0.0).astype(jnp.bfloat16), 9 * LANE, 18 * LANE)
    out = jnp.where(low, 0.0, a_last / t_last)
    attn[:, pl.ds(9 * LANE, LANE)] = pltpu.roll(out, HEAD, 1).astype(jnp.bfloat16)

    wait(w_o, sems.at[4])

    def out_block(c, width):
        proj = lax.dot_general(
            attn[...], w_o[pl.ds(c, width), :], contract, preferred_element_type=jnp.float32
        )
        xf = x_ref[:, pl.ds(c, width)].astype(jnp.float32)
        gate = mod_ref[2:3, pl.ds(c, width)]
        x_out[:, pl.ds(c, width)] = (xf + gate * proj).astype(jnp.bfloat16)

    def out_body(j, _):
        out_block(pl.multiple_of(j * NT, NT), NT)
        return 0

    lax.fori_loop(0, D // NT, out_body, 0)
    out_block((D // NT) * NT, D % NT)
    if final:
        norm_rows(x_out, fmod_ref.at[0:1, :], fmod_ref.at[1:2, :], normed)
        vel_ref[...] = jnp.dot(normed[...], fw_ref[...], preferred_element_type=jnp.float32)


def run_layer(scalars, x, mod, fmod, gain, fw, mine, theirs, stale, text, req, final):
    vmem = pl.BlockSpec(memory_space=pltpu.VMEM)
    hbm = pl.BlockSpec(memory_space=pl.ANY)
    first = (
        jax.ShapeDtypeStruct((ROWS, fw.shape[1]), jnp.float32)
        if final
        else jax.ShapeDtypeStruct((ROWS, D), jnp.bfloat16)
    )
    scratch = [
        pltpu.VMEM((D, D), jnp.bfloat16),
        pltpu.VMEM((D, ZC), jnp.bfloat16),
        pltpu.VMEM((D, ZC), jnp.bfloat16),
        pltpu.VMEM((KEYS, D), jnp.bfloat16),
        pltpu.VMEM((ROWS, D), jnp.bfloat16),
        pltpu.VMEM((ROWS, ZC), jnp.float32),
        pltpu.VMEM((ROWS, ZC), jnp.bfloat16),
        pltpu.VMEM((NT, NT), jnp.bfloat16),
        pltpu.SemaphoreType.DMA((5,)),
    ]
    if final:
        scratch.append(pltpu.VMEM((ROWS, D), jnp.bfloat16))
    return pl.pallas_call(
        lambda *refs: layer_kernel(final, req, *refs),
        name="last_layer" if final else "first_layer",
        out_shape=(first, jax.ShapeDtypeStruct((ROWS, D), jnp.bfloat16)),
        in_specs=[pl.BlockSpec(memory_space=pltpu.SMEM)] + [vmem] * 5 + [hbm] * 24,
        out_specs=(vmem, vmem),
        scratch_shapes=scratch,
        compiler_params=pltpu.CompilerParams(vmem_limit_bytes=56 << 20),
    )(scalars, x, mod, fmod, gain, fw, *mine, *theirs, *stale, text)


def on_device(
    hidden,
    text_kv,
    stale_kv,
    modulation,
    score_gain,
    qkv_weight,
    out_weight,
    final_mod,
    final_weight,
    latent,
    step_index,
):
    section = lax.axis_index("section")
    shard = lax.axis_index("shard")
    z_hi, x_at, core = shard // 8, (shard // 2) % 4, shard % 2

    qkv = qkv_weight[0]
    half_oq = jnp.concatenate([out_weight[0].T, qkv[:, :HW]], 1)
    both = jnp.stack([qkv[:, HW:], half_oq])
    got = core_flip(both)
    rows_of = jnp.where(core == 0, jnp.stack([both, got], 1), jnp.stack([got, both], 1))
    rows_of = rows_of.reshape(2, BLK, D)
    mine_block = jnp.where(core == 0, rows_of[0], rows_of[1])
    their_block = jnp.where(core == 0, rows_of[1], rows_of[0])
    near_z, near_x = mine_block[:, :ZC], mine_block[:, ZC:]

    opposite_z = z_flip(near_z)
    before_x, after_x = x_shift(near_x, 1), x_shift(near_x, -1)
    before_y, after_y = y_shift(stale_kv[0], 1), y_shift(stale_kv[0], -1)
    far_x = x_relay(jnp.where(core == 0, before_x, after_x))
    opposite_x3 = z_flip(jnp.concatenate([after(near_x, opposite_z), before_x, after_x], 0))
    pair_z = after(jnp.concatenate([near_z, opposite_z], 0), far_x)
    before_z, after_z = x_shift(pair_z, 1), x_shift(pair_z, -1)
    far_y = y_relay(jnp.where(core == 0, before_y, after_y))
    their_far_x = core_flip(after(far_x, before_y))
    their_before_x = core_flip(after(before_x, before_y))
    their_after_x = core_flip(after(after_x, before_y))
    far_z = x_relay(jnp.where(core == 0, before_z, after_z))
    opposite_far = z_flip(after(far_x, opposite_x3))
    their_opposite_z = core_flip(after(opposite_z, before_z))
    their_before_z = core_flip(before_z)
    their_after_z = core_flip(after_z)
    their_opposite_x3 = core_flip(opposite_x3)
    their_far_z = core_flip(far_z)
    their_opposite_far = core_flip(opposite_far)
    mine = (mine_block, opposite_z, before_z, after_z, far_z,
            before_x, after_x, far_x, opposite_x3, opposite_far)
    theirs = (their_block, their_opposite_z, their_before_z, their_after_z, their_far_z,
              their_before_x, their_after_x, their_far_x, their_opposite_x3, their_opposite_far)
    stale = (before_y, after_y, far_y)
    text = jnp.pad(text_kv[0], ((0, 0), (0, TXT_PAD - TXT), (0, 0)))
    gain = jnp.tile(score_gain[0] * (1.0 / math.sqrt(HEAD)), ZC // HEAD)[None, :]
    rows = [
        ((z_hi ^ slot) * 4 + (x_at + dx) % 4) * BLK for slot in range(2) for dx in (0, 3, 1, 2)
    ]
    scalars = jnp.stack([core, *rows]).astype(jnp.int32)

    def layer(x, r, final):
        return run_layer(
            scalars, x, modulation[0], final_mod, gain, final_weight,
            mine, theirs, stale, text, r, final,
        )

    fresh_first, arrived = [], []
    for r in range(2):
        x_next, fresh = layer(hidden, r, False)
        fresh_first.append(fresh)
        arrived.append(lax.ppermute(x_next, "section", [(0, 1)]))
    fresh_out, velocity = [], []
    for r in range(2):
        vel, fresh = layer(arrived[r], r, True)
        velocity.append(vel)
        fresh_out.append(jnp.where(section == 0, fresh_first[r], fresh))
    velocity = jnp.stack(velocity)
    half = latent.shape[1]
    sent = lax.ppermute(velocity[:, :half].astype(jnp.bfloat16), "section", [(1, 0)])
    velocity_mine = jnp.where(section == 0, sent.astype(jnp.float32), velocity[:, half:])
    sig = sigma_of(step_index)[:, None, None]
    sig_next = sigma_of(step_index + 1)[:, None, None]
    latent_next = latent + (sig_next - sig) * velocity_mine
    denoised = latent - sig * velocity_mine
    return (jnp.stack(fresh_out)[None], latent_next, denoised)


def solution(mesh):
    in_specs = (
        P("shard", "patch", None),
        P("section", "shard", None, None),
        P("section", "shard", "patch", None),
        P("section", "shard", None, None),
        P("section", None),
        P("section", "shard", None),
        P("section", None, "shard"),
        P("shard", None, None),
        P(),
        P("shard", ("patch", "section"), None),
        P("shard"),
    )
    out_specs = (
        P("section", "shard", "patch", None),
        P("shard", ("patch", "section"), None),
        P("shard", ("patch", "section"), None),
    )
    return jax.shard_map(
        on_device, mesh=mesh, in_specs=in_specs, out_specs=out_specs, check_vma=False
    )
```

```python
import math

import jax
import jax.numpy as jnp
from jax import lax
from jax.experimental import pallas as pl
from jax.experimental.pallas import tpu as pltpu
from jax.sharding import PartitionSpec as P

HEAD = 64
NSTEPS = 28
D = 2432
HW = 1216
ROWS = 256
TXT = 154
TXT_PAD = 160
KEYS = 4 * ROWS + TXT_PAD
BLK = 304
ZC = 1280
XC = D - ZC
LANE = 128
NT = 256

eps_norm = 1e-06
flow_shift = 3.0


def sigma_of(step):
    s = 1.0 - step.astype(jnp.float32) / NSTEPS
    return flow_shift * s / (1.0 + (flow_shift - 1.0) * s)


def shard_pairs(flip_z=0, dx=0, flip_core=0):
    pairs = []
    for z in range(2):
        for x in range(4):
            for c in range(2):
                src = z * 8 + x * 2 + c
                dst = (z ^ flip_z) * 8 + ((x + dx) % 4) * 2 + (c ^ flip_core)
                pairs.append((src, dst))
    return pairs


def ring_pairs(step):
    return [(i, (i + step) % 4) for i in range(4)]


def x_shift(value, dx):
    return lax.ppermute(value, "shard", shard_pairs(dx=dx))


def z_flip(value):
    return lax.ppermute(value, "shard", shard_pairs(flip_z=1))


def core_flip(value):
    return lax.ppermute(value, "shard", shard_pairs(flip_core=1))


def y_shift(value, dy):
    return lax.ppermute(value, "patch", ring_pairs(dy))


def x_relay(value):
    pairs = []
    for z in range(2):
        for x in range(4):
            for c in range(2):
                dx = 1 if c == 0 else -1
                pairs.append((z * 8 + x * 2 + c, z * 8 + ((x + dx) % 4) * 2 + c))
    return lax.ppermute(value, "shard", pairs)


def y_relay(value):
    pairs = []
    for y in range(4):
        for k in range(16):
            dy = 1 if k % 2 == 0 else -1
            pairs.append((y * 16 + k, ((y + dy) % 4) * 16 + k))
    return lax.ppermute(value, ("patch", "shard"), pairs)


def after(value, *earlier):
    return lax.optimization_barrier((value, *earlier))[0]


def group_scale(p, ones_ref):
    total = jnp.dot(
        (p * p).astype(jnp.bfloat16), ones_ref[...], preferred_element_type=jnp.float32
    )
    return lax.rsqrt(total * (1.0 / HEAD) + eps_norm)


def norm_rows(src_ref, shift_ref, scale_ref, dst_ref):
    step = 32

    def body(i, _):
        r = pl.multiple_of(i * step, step)
        xf = src_ref[pl.ds(r, step), :].astype(jnp.float32)
        mean = jnp.mean(xf, -1, keepdims=True)
        cent = xf - mean
        var = jnp.mean(cent * cent, -1, keepdims=True)
        out = cent * lax.rsqrt(var + eps_norm) * (1.0 + scale_ref[...]) + shift_ref[...]
        dst_ref[pl.ds(r, step), :] = out.astype(jnp.bfloat16)
        return 0

    lax.fori_loop(0, ROWS // step, body, 0)


def layer_kernel(final, req, *refs):
    sc, x_hbm, mod_ref, gain_ref = refs[:4]
    mine = refs[4:14]
    theirs = refs[14:24]
    stale = refs[24:27]
    text_ref = refs[27]
    refs = refs[28:]
    mod_ref = mod_ref.at[req]
    if final:
        fmod_ref, fw_ref, early_ref = refs[0].at[req], refs[1], refs[2]
        refs = refs[4:] if req else refs[3:]
        vel_ref, fresh_ref = refs[:2]
        fresh_ref = fresh_ref.at[req]
        w_kv, w_q, w_o, kv, normed, qbuf, attn, ones, x_ref, sems, x_out = refs[2:]
    else:
        x_hbm = x_hbm.at[req]
        x_out, fresh_ref = refs[:2]
        w_kv, w_q, w_o, kv, normed, qbuf, attn, ones, x_ref, sems = refs[2:]
    row_of = lambda slot, j: pl.multiple_of(sc[1 + slot * 4 + j], 16)

    def put(ref, at, cols, dst, slot, j, dst_cols, sem):
        pltpu.make_async_copy(
            ref.at[pl.ds(at, BLK), cols], dst.at[pl.ds(row_of(slot, j), BLK), dst_cols], sem
        ).start()

    def spread_z(pieces, cols, dst, dst_cols, sem):
        block, opposite = pieces[:2]
        put(block, 0, cols, dst, 0, 0, dst_cols, sem)
        put(opposite, 0, cols, dst, 1, 0, dst_cols, sem)
        for j, ref in enumerate(pieces[2:5]):
            for slot in range(2):
                put(ref, slot * BLK, cols, dst, slot, j + 1, dst_cols, sem)

    def spread_x(pieces, dst, dst_cols, sem):
        cols = pl.ds(0, XC)
        put(pieces[0], 0, pl.ds(ZC, XC), dst, 0, 0, dst_cols, sem)
        for j, ref in enumerate(pieces[5:8]):
            put(ref, 0, cols, dst, 0, j + 1, dst_cols, sem)
        for j in range(3):
            put(pieces[8], j * BLK, cols, dst, 1, j, dst_cols, sem)
        put(pieces[9], 0, cols, dst, 1, 3, dst_cols, sem)

    def by_core(step):
        @pl.when(sc[0] == 0)
        def _():
            step(mine, theirs)

        @pl.when(sc[0] != 0)
        def _():
            step(theirs, mine)

    def fetch_kv_z(kv_pieces, oq_pieces):
        spread_z(kv_pieces, pl.ds(0, ZC), w_kv, pl.ds(0, ZC), sems.at[0])

    def fetch_kv_x(kv_pieces, oq_pieces):
        spread_x(kv_pieces, w_kv, pl.ds(ZC, XC), sems.at[1])

    def fetch_q(kv_pieces, oq_pieces):
        spread_z(oq_pieces, pl.ds(0, ZC), w_q, pl.ds(0, ZC), sems.at[2])

    def fetch_out(kv_pieces, oq_pieces):
        spread_z(oq_pieces, pl.ds(ZC - LANE, LANE), w_o, pl.ds(0, LANE), sems.at[4])
        spread_x(oq_pieces, w_o, pl.ds(LANE, XC), sems.at[4])

    def fetch_keys():
        for j, ref in enumerate((*stale, text_ref)):
            count = ROWS if j < 3 else TXT_PAD
            pltpu.make_async_copy(
                ref.at[req], kv.at[pl.ds((j + 1) * ROWS, count), :], sems.at[3]
            ).start()

    def wait(dst, sem):
        pltpu.make_async_copy(dst, dst, sem).wait()

    pltpu.make_async_copy(x_hbm, x_ref, sems.at[5]).start()
    by_core(fetch_kv_z)
    wait(x_ref, sems.at[5])

    norm_rows(x_ref, mod_ref.at[0:1, :], mod_ref.at[1:2, :], normed)
    gi = lax.broadcasted_iota(jnp.int32, (NT, NT), 0) // HEAD
    gj = lax.broadcasted_iota(jnp.int32, (NT, NT), 1) // HEAD
    ones[...] = jnp.where(gi == gj, 1.0, 0.0).astype(jnp.bfloat16)

    by_core(fetch_kv_x)
    wait(w_kv.at[:, pl.ds(0, ZC)], sems.at[0])
    by_core(fetch_q)

    def key_block(j, _):
        c = pl.multiple_of(j * NT, NT)
        p = jnp.dot(normed[...], w_kv[:, pl.ds(c, NT)], preferred_element_type=jnp.float32)
        col = lax.broadcasted_iota(jnp.int32, (ROWS, NT), 1) + c
        out = (p * jnp.where(col < HW, group_scale(p, ones), 1.0)).astype(jnp.bfloat16)
        kv[pl.ds(0, ROWS), pl.ds(c, NT)] = out
        return 0

    lax.fori_loop(0, ZC // NT, key_block, 0)
    wait(w_kv.at[:, pl.ds(ZC, XC)], sems.at[1])
    fetch_keys()
    vw = 1152

    def value_block(j, _):
        c = pl.multiple_of(ZC + j * vw, LANE)
        p = jnp.dot(normed[...], w_kv[:, pl.ds(c, vw)], preferred_element_type=jnp.float32)
        out = p.astype(jnp.bfloat16)
        kv[pl.ds(0, ROWS), pl.ds(c, vw)] = out
        return 0

    lax.fori_loop(0, XC // vw, value_block, 0)
    new_rows = kv.at[pl.ds(0, ROWS), :]
    if final:

        @pl.when(sc[9] == 0)
        def _():
            pltpu.make_async_copy(early_ref, fresh_ref, sems.at[6]).start()

        @pl.when(sc[9] != 0)
        def _():
            pltpu.make_async_copy(new_rows, fresh_ref, sems.at[6]).start()

    else:
        pltpu.make_async_copy(new_rows, fresh_ref, sems.at[6]).start()
    wait(w_q, sems.at[2])
    by_core(fetch_out)

    def query_block(j, _):
        c = pl.multiple_of(j * NT, NT)
        p = jnp.dot(normed[...], w_q[:, pl.ds(c, NT)], preferred_element_type=jnp.float32)
        q = p * group_scale(p, ones) * gain_ref[:, pl.ds(c, NT)]
        qbuf[:, pl.ds(c, NT)] = q.astype(jnp.bfloat16)
        return 0

    lax.fori_loop(0, ZC // NT, query_block, 0)
    wait(kv.at[pl.ds(ROWS, KEYS - ROWS), :], sems.at[3])

    low = lax.broadcasted_iota(jnp.int32, (ROWS, LANE), 1) < HEAD
    zero = jnp.zeros((ROWS, LANE), jnp.bfloat16)
    chunks = [(i * ROWS, ROWS) for i in range(4)] + [(4 * ROWS, TXT_PAD)]
    contract = (((1,), (1,)), ((), ()))
    one_rows = jnp.ones((ROWS, LANE), jnp.bfloat16)
    text_rows = jnp.where(
        lax.broadcasted_iota(jnp.int32, (TXT_PAD, LANE), 0) < TXT, 1.0, 0.0
    ).astype(jnp.bfloat16)

    def attend(q, key_of, vc):
        acc = None
        for start, count in chunks:
            v = kv[pl.ds(start, count), pl.ds(vc, LANE)]
            s = lax.dot_general(
                q, key_of(start, count), contract, preferred_element_type=jnp.float32
            )
            w = jnp.exp(s).astype(jnp.bfloat16)
            v_one = jnp.concatenate([v, one_rows if count == ROWS else text_rows], 1)
            part = jnp.dot(w, v_one, preferred_element_type=jnp.float32)
            acc = part if acc is None else acc + part
        return acc[:, :LANE] / acc[:, LANE:]

    def pair(j, _):
        c = pl.multiple_of(j * LANE, LANE)
        n = pl.multiple_of(c + LANE, LANE)
        q_c, q_n = qbuf[:, pl.ds(c, LANE)], qbuf[:, pl.ds(n, LANE)]
        q = jnp.concatenate([jnp.where(low, zero, q_c), jnp.where(low, q_n, zero)], 0)

        def key_of(start, count):
            return jnp.where(
                low[:count], kv[pl.ds(start, count), pl.ds(n, LANE)],
                kv[pl.ds(start, count), pl.ds(c, LANE)],
            )

        out = attend(q, key_of, pl.multiple_of(c + 10 * LANE, LANE))
        out = jnp.where(low, out[:ROWS], out[ROWS:])
        attn[:, pl.ds(n, LANE)] = out.astype(jnp.bfloat16)
        return 0

    lax.fori_loop(0, 9, pair, 0, unroll=9)
    first = attend(
        jnp.where(low, qbuf[:, pl.ds(0, LANE)], zero),
        lambda start, count: kv[pl.ds(start, count), pl.ds(0, LANE)],
        9 * LANE,
    )
    attn[:, pl.ds(0, LANE)] = jnp.where(low, 0.0, first).astype(jnp.bfloat16)

    wait(w_o, sems.at[4])

    def out_block(c, width):
        proj = lax.dot_general(
            attn[...], w_o[pl.ds(c, width), :], contract, preferred_element_type=jnp.float32
        )
        xf = x_ref[:, pl.ds(c, width)].astype(jnp.float32)
        gate = mod_ref[2:3, pl.ds(c, width)]
        x_out[:, pl.ds(c, width)] = (xf + gate * proj).astype(jnp.bfloat16)

    def out_body(j, _):
        out_block(pl.multiple_of(j * NT, NT), NT)
        return 0

    lax.fori_loop(0, D // NT, out_body, 0)
    out_block((D // NT) * NT, D % NT)
    if final:
        norm_rows(x_out, fmod_ref.at[0:1, :], fmod_ref.at[1:2, :], normed)
        vel_ref[...] = jnp.dot(normed[...], fw_ref[...], preferred_element_type=jnp.float32)
    wait(new_rows, sems.at[6])


def run_layer(scalars, x, mod, gain, mine, theirs, stale, text, req, last=None):
    vmem = pl.BlockSpec(memory_space=pltpu.VMEM)
    hbm = pl.BlockSpec(memory_space=pl.ANY)
    final = last is not None
    operands = [scalars, x, mod, gain, *mine, *theirs, *stale, text]
    specs = [pl.BlockSpec(memory_space=pltpu.SMEM), hbm, vmem, vmem] + [hbm] * 24
    scratch = [
        pltpu.VMEM((D, D), jnp.bfloat16),
        pltpu.VMEM((D, ZC), jnp.bfloat16),
        pltpu.VMEM((D, ZC), jnp.bfloat16),
        pltpu.VMEM((KEYS, D), jnp.bfloat16),
        pltpu.VMEM((ROWS, D), jnp.bfloat16),
        pltpu.VMEM((ROWS, ZC), jnp.bfloat16),
        pltpu.VMEM((ROWS, ZC), jnp.bfloat16),
        pltpu.VMEM((NT, NT), jnp.bfloat16),
        pltpu.VMEM((ROWS, D), jnp.bfloat16),
        pltpu.SemaphoreType.DMA((7,)),
    ]
    aliases = {}
    if final:
        fmod, fw, early, new_kv = last
        operands += [fmod, fw, early]
        specs += [vmem, vmem, hbm]
        if req:
            aliases = {len(operands): 1}
            operands.append(new_kv)
            specs.append(hbm)
        outs = (
            jax.ShapeDtypeStruct((ROWS, fw.shape[1]), jnp.float32),
            jax.ShapeDtypeStruct((2, ROWS, D), jnp.bfloat16),
        )
        out_specs = (vmem, hbm)
        scratch.append(pltpu.VMEM((ROWS, D), jnp.bfloat16))
    else:
        outs = (jax.ShapeDtypeStruct((ROWS, D), jnp.bfloat16),) * 2
        out_specs = (vmem, hbm)
    return pl.pallas_call(
        lambda *refs: layer_kernel(final, req, *refs),
        name="last_layer" if final else "first_layer",
        out_shape=outs,
        in_specs=specs,
        out_specs=out_specs,
        scratch_shapes=scratch,
        input_output_aliases=aliases,
        compiler_params=pltpu.CompilerParams(vmem_limit_bytes=56 << 20),
    )(*operands)


def on_device(
    hidden,
    text_kv,
    stale_kv,
    modulation,
    score_gain,
    qkv_weight,
    out_weight,
    final_mod,
    final_weight,
    latent,
    step_index,
):
    section = lax.axis_index("section")
    shard = lax.axis_index("shard")
    z_hi, x_at, core = shard // 8, (shard // 2) % 4, shard % 2

    qkv = qkv_weight[0]
    half_oq = jnp.concatenate([qkv[:, :HW], out_weight[0].T], 1)
    both = jnp.stack([qkv[:, HW:], half_oq])
    got = core_flip(both)
    rows_of = jnp.where(core == 0, jnp.stack([both, got], 1), jnp.stack([got, both], 1))
    rows_of = rows_of.reshape(2, BLK, D)
    mine_block = jnp.where(core == 0, rows_of[0], rows_of[1])
    their_block = jnp.where(core == 0, rows_of[1], rows_of[0])
    near_z, near_x = mine_block[:, :ZC], mine_block[:, ZC:]

    opposite_z = z_flip(near_z)
    before_x, after_x = x_shift(near_x, 1), x_shift(near_x, -1)
    before_y, after_y = y_shift(stale_kv[0], 1), y_shift(stale_kv[0], -1)
    far_x = x_relay(jnp.where(core == 0, before_x, after_x))
    opposite_x3 = z_flip(jnp.concatenate([after(near_x, opposite_z), before_x, after_x], 0))
    pair_z = after(jnp.concatenate([near_z, opposite_z], 0), far_x)
    before_z, after_z = x_shift(pair_z, 1), x_shift(pair_z, -1)
    far_y = y_relay(jnp.where(core == 0, before_y, after_y))
    their_far_x = core_flip(after(far_x, before_y))
    their_before_x = core_flip(after(before_x, before_y))
    their_after_x = core_flip(after(after_x, before_y))
    far_z = x_relay(jnp.where(core == 0, before_z, after_z))
    opposite_far = z_flip(after(far_x, opposite_x3))
    their_opposite_z = core_flip(after(opposite_z, before_z))
    their_before_z = core_flip(before_z)
    their_after_z = core_flip(after_z)
    their_opposite_x3 = core_flip(opposite_x3)
    their_far_z = core_flip(far_z)
    their_opposite_far = core_flip(opposite_far)
    mine = (mine_block, opposite_z, before_z, after_z, far_z,
            before_x, after_x, far_x, opposite_x3, opposite_far)
    theirs = (their_block, their_opposite_z, their_before_z, their_after_z, their_far_z,
              their_before_x, their_after_x, their_far_x, their_opposite_x3, their_opposite_far)
    stale = (before_y, after_y, far_y)
    text = jnp.pad(text_kv[0], ((0, 0), (0, TXT_PAD - TXT), (0, 0)))
    gain = jnp.tile(score_gain[0] * (1.0 / math.sqrt(HEAD)), ZC // HEAD)[None, :]
    rows = [
        ((z_hi ^ slot) * 4 + (x_at + dx) % 4) * BLK for slot in range(2) for dx in (0, 3, 1, 2)
    ]
    scalars = jnp.stack([core, *rows, section]).astype(jnp.int32)

    def layer(x, r, last=None):
        return run_layer(
            scalars, x, modulation[0], gain, mine, theirs, stale, text, r, last
        )

    fresh_first, arrived = [], []
    for r in range(2):
        x_next, fresh = layer(hidden, r)
        fresh_first.append(fresh)
        arrived.append(lax.ppermute(x_next, "section", [(0, 1)]))
    velocity, new_kv = [], None
    for r in range(2):
        vel, new_kv = layer(arrived[r], r, (final_mod, final_weight, fresh_first[r], new_kv))
        velocity.append(vel)
    velocity = jnp.stack(velocity)
    half = latent.shape[1]
    sent = lax.ppermute(velocity[:, :half].astype(jnp.bfloat16), "section", [(1, 0)])
    velocity_mine = jnp.where(section == 0, sent.astype(jnp.float32), velocity[:, half:])
    sig = sigma_of(step_index)[:, None, None]
    sig_next = sigma_of(step_index + 1)[:, None, None]
    latent_next = latent + (sig_next - sig) * velocity_mine
    denoised = latent - sig * velocity_mine
    return (new_kv[None], latent_next, denoised)


def solution(mesh):
    in_specs = (
        P("shard", "patch", None),
        P("section", "shard", None, None),
        P("section", "shard", "patch", None),
        P("section", "shard", None, None),
        P("section", None),
        P("section", "shard", None),
        P("section", None, "shard"),
        P("shard", None, None),
        P(),
        P("shard", ("patch", "section"), None),
        P("shard"),
    )
    out_specs = (
        P("section", "shard", "patch", None),
        P("shard", ("patch", "section"), None),
        P("shard", ("patch", "section"), None),
    )
    return jax.shard_map(
        on_device, mesh=mesh, in_specs=in_specs, out_specs=out_specs, check_vma=False
    )
```

```python
import math

import jax
import jax.numpy as jnp
from jax import lax
from jax.experimental import pallas as pl
from jax.experimental.pallas import tpu as pltpu
from jax.sharding import PartitionSpec as P

HEAD = 64
NSTEPS = 28
D = 2432
HW = 1216
ROWS = 256
TXT = 154
TXT_PAD = 160
KEYS = 4 * ROWS + TXT_PAD
BLK = 304
ZC = 1152
XC = D - ZC
WIDE = 1280
LANE = 128
NT = 256

eps_norm = 1e-06
flow_shift = 3.0


def sigma_of(step):
    s = 1.0 - step.astype(jnp.float32) / NSTEPS
    return flow_shift * s / (1.0 + (flow_shift - 1.0) * s)


def shard_pairs(flip_z=0, dx=0, flip_core=0):
    pairs = []
    for z in range(2):
        for x in range(4):
            for c in range(2):
                src = z * 8 + x * 2 + c
                dst = (z ^ flip_z) * 8 + ((x + dx) % 4) * 2 + (c ^ flip_core)
                pairs.append((src, dst))
    return pairs


def ring_pairs(step):
    return [(i, (i + step) % 4) for i in range(4)]


def x_shift(value, dx):
    return lax.ppermute(value, "shard", shard_pairs(dx=dx))


def z_flip(value):
    return lax.ppermute(value, "shard", shard_pairs(flip_z=1))


def core_flip(value):
    return lax.ppermute(value, "shard", shard_pairs(flip_core=1))


def y_shift(value, dy):
    return lax.ppermute(value, "patch", ring_pairs(dy))


def x_relay(value):
    pairs = []
    for z in range(2):
        for x in range(4):
            for c in range(2):
                dx = 1 if c == 0 else -1
                pairs.append((z * 8 + x * 2 + c, z * 8 + ((x + dx) % 4) * 2 + c))
    return lax.ppermute(value, "shard", pairs)


def y_relay(value):
    pairs = []
    for y in range(4):
        for k in range(16):
            dy = 1 if k % 2 == 0 else -1
            pairs.append((y * 16 + k, ((y + dy) % 4) * 16 + k))
    return lax.ppermute(value, ("patch", "shard"), pairs)


def after(value, *earlier):
    return lax.optimization_barrier((value, *earlier))[0]


def group_scale(p, ones_ref):
    total = jnp.dot(
        (p * p).astype(jnp.bfloat16), ones_ref[...], preferred_element_type=jnp.float32
    )
    return lax.rsqrt(total * (1.0 / HEAD) + eps_norm)


def norm_rows(src_ref, shift_ref, scale_ref, dst_ref):
    step = 32

    def body(i, _):
        r = pl.multiple_of(i * step, step)
        xf = src_ref[pl.ds(r, step), :].astype(jnp.float32)
        mean = jnp.mean(xf, -1, keepdims=True)
        cent = xf - mean
        var = jnp.mean(cent * cent, -1, keepdims=True)
        out = cent * lax.rsqrt(var + eps_norm) * (1.0 + scale_ref[...]) + shift_ref[...]
        dst_ref[pl.ds(r, step), :] = out.astype(jnp.bfloat16)
        return 0

    lax.fori_loop(0, ROWS // step, body, 0)


def layer_kernel(final, req, *refs):
    sc, x_hbm, mod_ref, gain_ref = refs[:4]
    mine = refs[4:13]
    theirs = refs[13:22]
    stale = refs[22:25]
    text_ref = refs[25]
    refs = refs[26:]
    mod_ref = mod_ref.at[req]
    if final:
        fmod_ref, fw_ref, early_ref = refs[0].at[req], refs[1], refs[2]
        refs = refs[4:] if req else refs[3:]
        vel_ref, fresh_ref = refs[:2]
        fresh_ref = fresh_ref.at[req]
        w_kv, w_q, w_o, kv, normed, qbuf, attn, ones, x_ref, sems, x_out = refs[2:]
    else:
        x_hbm = x_hbm.at[req]
        x_out, fresh_ref = refs[:2]
        w_kv, w_q, w_o, kv, normed, qbuf, attn, ones, x_ref, sems = refs[2:]
    row_of = lambda slot, j: pl.multiple_of(sc[1 + slot * 4 + j], 16)

    def put(ref, at, col, count, dst, slot, j, dst_col, sem):
        pltpu.make_async_copy(
            ref.at[pl.ds(at, BLK), pl.ds(col, count)],
            dst.at[pl.ds(row_of(slot, j), BLK), pl.ds(dst_col, count)],
            sem,
        ).start()

    def spread_z(pieces, dst, sem):
        put(pieces[0], 0, 0, ZC, dst, 0, 0, 0, sem)
        put(pieces[1], 0, 0, ZC, dst, 1, 0, 0, sem)
        for j, ref in enumerate(pieces[4:7]):
            for slot in range(2):
                put(ref, slot * BLK, 0, ZC, dst, slot, j + 1, 0, sem)

    def spread_x(pieces, count, dst, dst_col, sem):
        for slot in range(2):
            near, two, far = pieces[slot], pieces[(2, 7)[slot]], pieces[(3, 8)[slot]]
            put(near, 0, ZC, count, dst, slot, 0, dst_col, sem)
            for j in range(2):
                put(two, j * BLK, 0, count, dst, slot, j + 1, dst_col, sem)
            put(far, 0, 0, count, dst, slot, 3, dst_col, sem)

    def by_core(step):
        @pl.when(sc[0] == 0)
        def _():
            step(mine, theirs)

        @pl.when(sc[0] != 0)
        def _():
            step(theirs, mine)

    def fetch_kv_z(kv_pieces, oq_pieces):
        spread_z(kv_pieces, w_kv, sems.at[0])

    def fetch_kv_x(kv_pieces, oq_pieces):
        spread_x(kv_pieces, XC, w_kv, ZC, sems.at[1])

    def fetch_q(kv_pieces, oq_pieces):
        spread_z(oq_pieces, w_q, sems.at[2])
        spread_x(oq_pieces, WIDE - ZC, w_q, ZC, sems.at[2])

    def fetch_out(kv_pieces, oq_pieces):
        spread_x(oq_pieces, XC, w_o, 0, sems.at[4])

    def fetch_keys():
        for j, ref in enumerate((*stale, text_ref)):
            count = ROWS if j < 3 else TXT_PAD
            pltpu.make_async_copy(
                ref.at[req], kv.at[pl.ds((j + 1) * ROWS, count), :], sems.at[3]
            ).start()

    def wait(dst, sem):
        pltpu.make_async_copy(dst, dst, sem).wait()

    pltpu.make_async_copy(x_hbm, x_ref, sems.at[5]).start()
    by_core(fetch_kv_z)
    wait(x_ref, sems.at[5])

    norm_rows(x_ref, mod_ref.at[0:1, :], mod_ref.at[1:2, :], normed)
    gi = lax.broadcasted_iota(jnp.int32, (NT, NT), 0) // HEAD
    gj = lax.broadcasted_iota(jnp.int32, (NT, NT), 1) // HEAD
    ones[...] = jnp.where(gi == gj, 1.0, 0.0).astype(jnp.bfloat16)

    by_core(fetch_kv_x)
    wait(w_kv.at[:, pl.ds(0, ZC)], sems.at[0])
    by_core(fetch_q)

    def key_block(j, _):
        c = pl.multiple_of(j * NT, NT)
        p = jnp.dot(normed[...], w_kv[:, pl.ds(c, NT)], preferred_element_type=jnp.float32)
        col = lax.broadcasted_iota(jnp.int32, (ROWS, NT), 1) + c
        out = p * jnp.where(col < HW, group_scale(p, ones), 1.0)
        kv[pl.ds(0, ROWS), pl.ds(c, NT)] = out.astype(jnp.bfloat16)
        return 0

    lax.fori_loop(0, ZC // NT, key_block, 0)
    wait(w_kv.at[:, pl.ds(ZC, XC)], sems.at[1])
    fetch_keys()
    key_block(ZC // NT, 0)
    vw = 384

    def value_block(j, _):
        c = pl.multiple_of(WIDE + j * vw, LANE)
        p = jnp.dot(normed[...], w_kv[:, pl.ds(c, vw)], preferred_element_type=jnp.float32)
        kv[pl.ds(0, ROWS), pl.ds(c, vw)] = p.astype(jnp.bfloat16)
        return 0

    lax.fori_loop(0, (D - WIDE) // vw, value_block, 0)
    new_rows = kv.at[pl.ds(0, ROWS), :]
    spare = w_kv.at[pl.ds(0, ROWS), :]
    if final:

        @pl.when(sc[9] == 0)
        def _():
            pltpu.make_async_copy(early_ref, spare, sems.at[6]).start()

    else:
        pltpu.make_async_copy(new_rows, fresh_ref, sems.at[6]).start()
    wait(w_q, sems.at[2])
    by_core(fetch_out)

    def query_block(j, _):
        c = pl.multiple_of(j * NT, NT)
        p = jnp.dot(normed[...], w_q[:, pl.ds(c, NT)], preferred_element_type=jnp.float32)
        q = p * group_scale(p, ones) * gain_ref[:, pl.ds(c, NT)]
        qbuf[:, pl.ds(c, NT)] = q.astype(jnp.bfloat16)
        return 0

    lax.fori_loop(0, WIDE // NT, query_block, 0)
    wait(kv.at[pl.ds(ROWS, KEYS - ROWS), :], sems.at[3])

    low = lax.broadcasted_iota(jnp.int32, (ROWS, LANE), 1) < HEAD
    zero = jnp.zeros((ROWS, LANE), jnp.bfloat16)
    chunks = [(i * ROWS, ROWS) for i in range(4)] + [(4 * ROWS, TXT_PAD)]
    contract = (((1,), (1,)), ((), ()))
    one_rows = jnp.ones((ROWS, LANE), jnp.bfloat16)
    text_rows = jnp.where(
        lax.broadcasted_iota(jnp.int32, (TXT_PAD, LANE), 0) < TXT, 1.0, 0.0
    ).astype(jnp.bfloat16)

    def attend(q, key_of, vc):
        acc = None
        for start, count in chunks:
            v = kv[pl.ds(start, count), pl.ds(vc, LANE)]
            s = lax.dot_general(
                q, key_of(start, count), contract, preferred_element_type=jnp.float32
            )
            w = jnp.exp(s).astype(jnp.bfloat16)
            v_one = jnp.concatenate([v, one_rows if count == ROWS else text_rows], 1)
            part = jnp.dot(w, v_one, preferred_element_type=jnp.float32)
            acc = part if acc is None else acc + part
        return acc[:, :LANE] / acc[:, LANE:]

    def pair(j, _):
        c = pl.multiple_of(j * LANE, LANE)
        n = pl.multiple_of(c + LANE, LANE)
        q_c, q_n = qbuf[:, pl.ds(c, LANE)], qbuf[:, pl.ds(n, LANE)]
        q = jnp.concatenate([jnp.where(low, zero, q_c), jnp.where(low, q_n, zero)], 0)

        def key_of(start, count):
            return jnp.where(
                low[:count], kv[pl.ds(start, count), pl.ds(n, LANE)],
                kv[pl.ds(start, count), pl.ds(c, LANE)],
            )

        out = attend(q, key_of, pl.multiple_of(c + 10 * LANE, LANE))
        out = jnp.where(low, out[:ROWS], out[ROWS:])
        attn[:, pl.ds(n, LANE)] = out.astype(jnp.bfloat16)
        return 0

    lax.fori_loop(0, 9, pair, 0, unroll=3)
    first = attend(
        jnp.where(low, qbuf[:, pl.ds(0, LANE)], zero),
        lambda start, count: kv[pl.ds(start, count), pl.ds(0, LANE)],
        9 * LANE,
    )
    attn[:, pl.ds(0, LANE)] = jnp.where(low, 0.0, first).astype(jnp.bfloat16)

    if final:

        @pl.when(sc[9] == 0)
        def _():
            wait(spare, sems.at[6])
            pltpu.make_async_copy(spare, fresh_ref, sems.at[6]).start()

        @pl.when(sc[9] != 0)
        def _():
            pltpu.make_async_copy(new_rows, fresh_ref, sems.at[6]).start()

    wait(w_o, sems.at[4])

    def out_block(c, width):
        proj = lax.dot_general(
            attn[...], w_o[pl.ds(c, width), :], contract, preferred_element_type=jnp.float32
        )
        xf = x_ref[:, pl.ds(c, width)].astype(jnp.float32)
        gate = mod_ref[2:3, pl.ds(c, width)]
        x_out[:, pl.ds(c, width)] = (xf + gate * proj).astype(jnp.bfloat16)

    def out_body(j, _):
        out_block(pl.multiple_of(j * NT, NT), NT)
        return 0

    lax.fori_loop(0, D // NT, out_body, 0)
    out_block((D // NT) * NT, D % NT)
    if final:
        norm_rows(x_out, fmod_ref.at[0:1, :], fmod_ref.at[1:2, :], normed)
        vel_ref[...] = jnp.dot(normed[...], fw_ref[...], preferred_element_type=jnp.float32)
    wait(new_rows, sems.at[6])


def run_layer(scalars, x, mod, gain, mine, theirs, stale, text, req, last=None):
    vmem = pl.BlockSpec(memory_space=pltpu.VMEM)
    hbm = pl.BlockSpec(memory_space=pl.ANY)
    final = last is not None
    operands = [scalars, x, mod, gain, *mine, *theirs, *stale, text]
    specs = [pl.BlockSpec(memory_space=pltpu.SMEM), hbm, vmem, vmem] + [hbm] * 22
    scratch = [
        pltpu.VMEM((D, D), jnp.bfloat16),
        pltpu.VMEM((D, WIDE), jnp.bfloat16),
        pltpu.VMEM((D, WIDE), jnp.bfloat16),
        pltpu.VMEM((KEYS, D), jnp.bfloat16),
        pltpu.VMEM((ROWS, D), jnp.bfloat16),
        pltpu.VMEM((ROWS, WIDE), jnp.bfloat16),
        pltpu.VMEM((ROWS, WIDE), jnp.bfloat16),
        pltpu.VMEM((NT, NT), jnp.bfloat16),
        pltpu.VMEM((ROWS, D), jnp.bfloat16),
        pltpu.SemaphoreType.DMA((7,)),
    ]
    aliases = {}
    if final:
        fmod, fw, early, new_kv = last
        operands += [fmod, fw, early]
        specs += [vmem, vmem, hbm]
        if req:
            aliases = {len(operands): 1}
            operands.append(new_kv)
            specs.append(hbm)
        outs = (
            jax.ShapeDtypeStruct((ROWS, fw.shape[1]), jnp.float32),
            jax.ShapeDtypeStruct((2, ROWS, D), jnp.bfloat16),
        )
        out_specs = (vmem, hbm)
        scratch.append(pltpu.VMEM((ROWS, D), jnp.bfloat16))
    else:
        outs = (jax.ShapeDtypeStruct((ROWS, D), jnp.bfloat16),) * 2
        out_specs = (vmem, hbm)
    return pl.pallas_call(
        lambda *refs: layer_kernel(final, req, *refs),
        name="last_layer" if final else "first_layer",
        out_shape=outs,
        in_specs=specs,
        out_specs=out_specs,
        scratch_shapes=scratch,
        input_output_aliases=aliases,
        compiler_params=pltpu.CompilerParams(vmem_limit_bytes=56 << 20),
    )(*operands)


def on_device(
    hidden,
    text_kv,
    stale_kv,
    modulation,
    score_gain,
    qkv_weight,
    out_weight,
    final_mod,
    final_weight,
    latent,
    step_index,
):
    section = lax.axis_index("section")
    shard = lax.axis_index("shard")
    z_hi, x_at, core = shard // 8, (shard // 2) % 4, shard % 2

    qkv = qkv_weight[0]
    half_kv = qkv[:, HW:]
    half_oq = jnp.concatenate([qkv[:, :HW], out_weight[0].T], 1)
    keep = jnp.where(core == 0, half_kv, half_oq)
    got = core_flip(jnp.where(core == 0, half_oq, half_kv))
    mine_block = jnp.concatenate(
        [jnp.where(core == 0, keep, got), jnp.where(core == 0, got, keep)], 0
    )
    near_z, near_x = mine_block[:, :ZC], mine_block[:, ZC:]
    text = jnp.pad(text_kv[0], ((0, 0), (0, TXT_PAD - TXT), (0, 0)))

    before_y, after_y = y_shift(stale_kv[0], 1), y_shift(stale_kv[0], -1)
    before_x, after_x = x_shift(near_x, 1), x_shift(near_x, -1)
    opposite = z_flip(mine_block)
    far_x = x_relay(jnp.where(core == 0, after(before_x, text), after_x))
    pair_z = jnp.concatenate([near_z, after(opposite, far_x)[:, :ZC]], 0)
    before_z, after_z = x_shift(pair_z, 1), x_shift(pair_z, -1)
    two_x = after(jnp.concatenate([before_x, after_x], 0), opposite)
    opposite_two = z_flip(two_x)
    far_y = y_relay(jnp.where(core == 0, before_y, after_y))
    far_z = x_relay(jnp.where(core == 0, before_z, after_z))
    opposite_far = z_flip(after(far_x, opposite_two))
    early = (mine_block, opposite, two_x, far_x)
    their_early = tuple(core_flip(after(piece, before_z)) for piece in early)
    their_before_z = core_flip(after(before_z, opposite_two))
    their_after_z = core_flip(after(after_z, opposite_two))
    their_opposite_two = core_flip(opposite_two)
    their_far_z = core_flip(far_z)
    their_opposite_far = core_flip(opposite_far)
    mine = (*early, before_z, after_z, far_z, opposite_two, opposite_far)
    theirs = (*their_early, their_before_z, their_after_z, their_far_z,
              their_opposite_two, their_opposite_far)
    stale = (before_y, after_y, far_y)
    gain = jnp.tile(score_gain[0] * (1.0 / math.sqrt(HEAD)), WIDE // HEAD)[None, :]
    rows = [
        ((z_hi ^ slot) * 4 + (x_at + dx) % 4) * BLK for slot in range(2) for dx in (0, 3, 1, 2)
    ]
    scalars = jnp.stack([core, *rows, section]).astype(jnp.int32)

    def layer(x, r, last=None):
        return run_layer(
            scalars, x, modulation[0], gain, mine, theirs, stale, text, r, last
        )

    fresh_first, arrived = [], []
    for r in range(2):
        x_next, fresh = layer(hidden, r)
        fresh_first.append(fresh)
        arrived.append(lax.ppermute(x_next, "section", [(0, 1)]))
    velocity, new_kv = [], None
    for r in range(2):
        vel, new_kv = layer(arrived[r], r, (final_mod, final_weight, fresh_first[r], new_kv))
        velocity.append(vel)
    velocity = jnp.stack(velocity)
    half = latent.shape[1]
    sent = lax.ppermute(velocity[:, :half].astype(jnp.bfloat16), "section", [(1, 0)])
    velocity_mine = jnp.where(section == 0, sent.astype(jnp.float32), velocity[:, half:])
    sig = sigma_of(step_index)[:, None, None]
    sig_next = sigma_of(step_index + 1)[:, None, None]
    latent_next = latent + (sig_next - sig) * velocity_mine
    denoised = latent - sig * velocity_mine
    return (new_kv[None], latent_next, denoised)


def solution(mesh):
    in_specs = (
        P("shard", "patch", None),
        P("section", "shard", None, None),
        P("section", "shard", "patch", None),
        P("section", "shard", None, None),
        P("section", None),
        P("section", "shard", None),
        P("section", None, "shard"),
        P("shard", None, None),
        P(),
        P("shard", ("patch", "section"), None),
        P("shard"),
    )
    out_specs = (
        P("section", "shard", "patch", None),
        P("shard", ("patch", "section"), None),
        P("shard", ("patch", "section"), None),
    )
    return jax.shard_map(
        on_device, mesh=mesh, in_specs=in_specs, out_specs=out_specs, check_vma=False
    )
```

```python
import math

import jax
import jax.numpy as jnp
from jax import lax
from jax.experimental import pallas as pl
from jax.experimental.pallas import tpu as pltpu
from jax.sharding import PartitionSpec as P

HEAD = 64
NSTEPS = 28
D = 2432
HW = 1216
ROWS = 256
TXT = 154
TXT_PAD = 160
KEYS = 4 * ROWS + TXT_PAD
BLK = 304
ZC = 1408
XC = D - ZC
WIDE = 1280
LANE = 128
NT = 256

eps_norm = 1e-06
flow_shift = 3.0


def sigma_of(step):
    s = 1.0 - step.astype(jnp.float32) / NSTEPS
    return flow_shift * s / (1.0 + (flow_shift - 1.0) * s)


def shard_pairs(flip_z=0, dx=0, flip_core=0):
    pairs = []
    for z in range(2):
        for x in range(4):
            for c in range(2):
                src = z * 8 + x * 2 + c
                dst = (z ^ flip_z) * 8 + ((x + dx) % 4) * 2 + (c ^ flip_core)
                pairs.append((src, dst))
    return pairs


def ring_pairs(step):
    return [(i, (i + step) % 4) for i in range(4)]


def x_shift(value, dx):
    return lax.ppermute(value, "shard", shard_pairs(dx=dx))


def z_flip(value):
    return lax.ppermute(value, "shard", shard_pairs(flip_z=1))


def core_flip(value):
    return lax.ppermute(value, "shard", shard_pairs(flip_core=1))


def y_shift(value, dy):
    return lax.ppermute(value, "patch", ring_pairs(dy))


def x_relay(value):
    pairs = []
    for z in range(2):
        for x in range(4):
            for c in range(2):
                dx = 1 if c == 0 else -1
                pairs.append((z * 8 + x * 2 + c, z * 8 + ((x + dx) % 4) * 2 + c))
    return lax.ppermute(value, "shard", pairs)


def y_relay(value):
    pairs = []
    for y in range(4):
        for k in range(16):
            dy = 1 if k % 2 == 0 else -1
            pairs.append((y * 16 + k, ((y + dy) % 4) * 16 + k))
    return lax.ppermute(value, ("patch", "shard"), pairs)


def after(value, *earlier):
    return lax.optimization_barrier((value, *earlier))[0]


def group_scale(p, ones_ref):
    total = jnp.dot(
        (p * p).astype(jnp.bfloat16), ones_ref[...], preferred_element_type=jnp.float32
    )
    return lax.rsqrt(total * (1.0 / HEAD) + eps_norm)


def norm_rows(src_ref, shift_ref, scale_ref, dst_ref):
    step = 32

    def body(i, _):
        r = pl.multiple_of(i * step, step)
        xf = src_ref[pl.ds(r, step), :].astype(jnp.float32)
        mean = jnp.mean(xf, -1, keepdims=True)
        cent = xf - mean
        var = jnp.mean(cent * cent, -1, keepdims=True)
        out = cent * lax.rsqrt(var + eps_norm) * (1.0 + scale_ref[...]) + shift_ref[...]
        dst_ref[pl.ds(r, step), :] = out.astype(jnp.bfloat16)
        return 0

    lax.fori_loop(0, ROWS // step, body, 0)


def layer_kernel(final, req, *refs):
    sc, x_hbm, mod_ref, gain_ref = refs[:4]
    mine = refs[4:13]
    theirs = refs[13:22]
    stale = refs[22:25]
    text_ref = refs[25]
    refs = refs[26:]
    mod_ref = mod_ref.at[req]
    if final:
        fmod_ref, fw_ref, early_ref = refs[0].at[req], refs[1], refs[2]
        refs = refs[4:] if req else refs[3:]
        low_ref, fresh_ref, high_ref = refs[:3]
        fresh_ref = fresh_ref.at[req]
        w_kv, w_q, w_o, kv, normed, qbuf, attn, ones, x_ref, sems, x_out = refs[3:]
    else:
        x_hbm = x_hbm.at[req]
        x_out, fresh_ref = refs[:2]
        w_kv, w_q, w_o, kv, normed, qbuf, attn, ones, x_ref, sems = refs[2:]
    row_of = lambda slot, j: pl.multiple_of(sc[1 + slot * 4 + j], 16)

    def put(ref, at, col, count, dst, slot, j, dst_col, sem):
        pltpu.make_async_copy(
            ref.at[pl.ds(at, BLK), pl.ds(col, count)],
            dst.at[pl.ds(row_of(slot, j), BLK), pl.ds(dst_col, count)],
            sem,
        ).start()

    def spread_z(pieces, col, count, dst, dst_col, sem):
        put(pieces[0], 0, col, count, dst, 0, 0, dst_col, sem)
        put(pieces[1], 0, col, count, dst, 1, 0, dst_col, sem)
        for j, ref in enumerate(pieces[4:7]):
            for slot in range(2):
                put(ref, slot * BLK, col, count, dst, slot, j + 1, dst_col, sem)

    def spread_x(pieces, dst, dst_col, sem):
        for slot in range(2):
            three, far = pieces[(2, 7)[slot]], pieces[(3, 8)[slot]]
            for j in range(3):
                put(three, j * BLK, 0, XC, dst, slot, j, dst_col, sem)
            put(far, 0, 0, XC, dst, slot, 3, dst_col, sem)

    def by_core(step):
        @pl.when(sc[0] == 0)
        def _():
            step(mine, theirs)

        @pl.when(sc[0] != 0)
        def _():
            step(theirs, mine)

    def fetch_kv_z(kv_pieces, oq_pieces):
        spread_z(kv_pieces, 0, ZC, w_kv, 0, sems.at[0])

    def fetch_kv_x(kv_pieces, oq_pieces):
        spread_x(kv_pieces, w_kv, ZC, sems.at[1])

    def fetch_q(kv_pieces, oq_pieces):
        spread_z(oq_pieces, 0, WIDE, w_q, 0, sems.at[2])

    def fetch_out(kv_pieces, oq_pieces):
        spread_z(oq_pieces, D - WIDE, ZC + WIDE - D, w_o, 0, sems.at[4])
        spread_x(oq_pieces, w_o, ZC + WIDE - D, sems.at[4])

    def fetch_keys():
        for j, ref in enumerate((*stale, text_ref)):
            count = ROWS if j < 3 else TXT_PAD
            pltpu.make_async_copy(
                ref.at[req], kv.at[pl.ds((j + 1) * ROWS, count), :], sems.at[3]
            ).start()

    def wait(dst, sem):
        pltpu.make_async_copy(dst, dst, sem).wait()

    pltpu.make_async_copy(x_hbm, x_ref, sems.at[5]).start()
    by_core(fetch_kv_z)
    wait(x_ref, sems.at[5])

    norm_rows(x_ref, mod_ref.at[0:1, :], mod_ref.at[1:2, :], normed)
    gi = lax.broadcasted_iota(jnp.int32, (NT, NT), 0) // HEAD
    gj = lax.broadcasted_iota(jnp.int32, (NT, NT), 1) // HEAD
    ones[...] = jnp.where(gi == gj, 1.0, 0.0).astype(jnp.bfloat16)

    by_core(fetch_kv_x)
    wait(w_kv.at[:, pl.ds(0, ZC)], sems.at[0])
    by_core(fetch_q)

    def key_block(j, _):
        c = pl.multiple_of(j * NT, NT)
        p = jnp.dot(normed[...], w_kv[:, pl.ds(c, NT)], preferred_element_type=jnp.float32)
        col = lax.broadcasted_iota(jnp.int32, (ROWS, NT), 1) + c
        out = p * jnp.where(col < HW, group_scale(p, ones), 1.0)
        kv[pl.ds(0, ROWS), pl.ds(c, NT)] = out.astype(jnp.bfloat16)
        return 0

    lax.fori_loop(0, WIDE // NT, key_block, 0)
    wait(w_kv.at[:, pl.ds(ZC, XC)], sems.at[1])
    fetch_keys()
    vw = 384

    def value_block(j, _):
        c = pl.multiple_of(WIDE + j * vw, LANE)
        p = jnp.dot(normed[...], w_kv[:, pl.ds(c, vw)], preferred_element_type=jnp.float32)
        kv[pl.ds(0, ROWS), pl.ds(c, vw)] = p.astype(jnp.bfloat16)
        return 0

    lax.fori_loop(0, (D - WIDE) // vw, value_block, 0)
    new_rows = kv.at[pl.ds(0, ROWS), :]
    spare = w_kv.at[pl.ds(0, ROWS), :]
    if final:

        @pl.when(sc[9] == 0)
        def _():
            pltpu.make_async_copy(early_ref, spare, sems.at[6]).start()

    else:
        pltpu.make_async_copy(new_rows, fresh_ref, sems.at[6]).start()
    wait(w_q, sems.at[2])
    by_core(fetch_out)

    def query_block(j, _):
        c = pl.multiple_of(j * NT, NT)
        p = jnp.dot(normed[...], w_q[:, pl.ds(c, NT)], preferred_element_type=jnp.float32)
        q = p * group_scale(p, ones) * gain_ref[:, pl.ds(c, NT)]
        qbuf[:, pl.ds(c, NT)] = q.astype(jnp.bfloat16)
        return 0

    lax.fori_loop(0, WIDE // NT, query_block, 0)
    wait(kv.at[pl.ds(ROWS, KEYS - ROWS), :], sems.at[3])

    low = lax.broadcasted_iota(jnp.int32, (ROWS, LANE), 1) < HEAD
    zero = jnp.zeros((ROWS, LANE), jnp.bfloat16)
    chunks = [(i * ROWS, ROWS) for i in range(4)] + [(4 * ROWS, TXT_PAD)]
    contract = (((1,), (1,)), ((), ()))
    one_rows = jnp.ones((ROWS, LANE), jnp.bfloat16)
    text_rows = jnp.where(
        lax.broadcasted_iota(jnp.int32, (TXT_PAD, LANE), 0) < TXT, 1.0, 0.0
    ).astype(jnp.bfloat16)

    def attend(q, key_of, vc):
        acc = None
        for start, count in chunks:
            v = kv[pl.ds(start, count), pl.ds(vc, LANE)]
            s = lax.dot_general(
                q, key_of(start, count), contract, preferred_element_type=jnp.float32
            )
            w = jnp.exp(s).astype(jnp.bfloat16)
            v_one = jnp.concatenate([v, one_rows if count == ROWS else text_rows], 1)
            part = jnp.dot(w, v_one, preferred_element_type=jnp.float32)
            acc = part if acc is None else acc + part
        return acc[:, :LANE] / acc[:, LANE:]

    def pair(j, _):
        c = pl.multiple_of(j * LANE, LANE)
        n = pl.multiple_of(c + LANE, LANE)
        q_c, q_n = qbuf[:, pl.ds(c, LANE)], qbuf[:, pl.ds(n, LANE)]
        q = jnp.concatenate([jnp.where(low, zero, q_c), jnp.where(low, q_n, zero)], 0)

        def key_of(start, count):
            return jnp.where(
                low[:count], kv[pl.ds(start, count), pl.ds(n, LANE)],
                kv[pl.ds(start, count), pl.ds(c, LANE)],
            )

        out = attend(q, key_of, pl.multiple_of(c + 10 * LANE, LANE))
        out = jnp.where(low, out[:ROWS], out[ROWS:])
        attn[:, pl.ds(n, LANE)] = out.astype(jnp.bfloat16)
        return 0

    lax.fori_loop(0, 9, pair, 0, unroll=3)
    first = attend(
        jnp.where(low, qbuf[:, pl.ds(0, LANE)], zero),
        lambda start, count: kv[pl.ds(start, count), pl.ds(0, LANE)],
        9 * LANE,
    )
    attn[:, pl.ds(0, LANE)] = jnp.where(low, 0.0, first).astype(jnp.bfloat16)

    if final:

        @pl.when(sc[9] == 0)
        def _():
            wait(spare, sems.at[6])
            pltpu.make_async_copy(spare, fresh_ref, sems.at[6]).start()

        @pl.when(sc[9] != 0)
        def _():
            pltpu.make_async_copy(new_rows, fresh_ref, sems.at[6]).start()

    wait(w_o, sems.at[4])

    def out_block(c, width):
        proj = lax.dot_general(
            attn[...], w_o[pl.ds(c, width), :], contract, preferred_element_type=jnp.float32
        )
        xf = x_ref[:, pl.ds(c, width)].astype(jnp.float32)
        gate = mod_ref[2:3, pl.ds(c, width)]
        x_out[:, pl.ds(c, width)] = (xf + gate * proj).astype(jnp.bfloat16)

    def out_body(j, _):
        out_block(pl.multiple_of(j * NT, NT), NT)
        return 0

    lax.fori_loop(0, D // NT, out_body, 0)
    out_block((D // NT) * NT, D % NT)
    if final:
        norm_rows(x_out, fmod_ref.at[0:1, :], fmod_ref.at[1:2, :], normed)
        vel = jnp.dot(normed[...], fw_ref[...], preferred_element_type=jnp.float32)
        half = ROWS // 2
        low_ref[...] = vel[:half].astype(jnp.bfloat16)
        high_ref[...] = vel[half:]
    wait(new_rows, sems.at[6])


def run_layer(scalars, x, mod, gain, mine, theirs, stale, text, req, last=None):
    vmem = pl.BlockSpec(memory_space=pltpu.VMEM)
    hbm = pl.BlockSpec(memory_space=pl.ANY)
    final = last is not None
    operands = [scalars, x, mod, gain, *mine, *theirs, *stale, text]
    specs = [pl.BlockSpec(memory_space=pltpu.SMEM), hbm, vmem, vmem] + [hbm] * 22
    scratch = [
        pltpu.VMEM((D, D), jnp.bfloat16),
        pltpu.VMEM((D, WIDE), jnp.bfloat16),
        pltpu.VMEM((D, WIDE), jnp.bfloat16),
        pltpu.VMEM((KEYS, D), jnp.bfloat16),
        pltpu.VMEM((ROWS, D), jnp.bfloat16),
        pltpu.VMEM((ROWS, WIDE), jnp.bfloat16),
        pltpu.VMEM((ROWS, WIDE), jnp.bfloat16),
        pltpu.VMEM((NT, NT), jnp.bfloat16),
        pltpu.VMEM((ROWS, D), jnp.bfloat16),
        pltpu.SemaphoreType.DMA((7,)),
    ]
    aliases = {}
    if final:
        fmod, fw, early, new_kv = last
        operands += [fmod, fw, early]
        specs += [vmem, vmem, hbm]
        if req:
            aliases = {len(operands): 1}
            operands.append(new_kv)
            specs.append(hbm)
        outs = (
            jax.ShapeDtypeStruct((ROWS // 2, fw.shape[1]), jnp.bfloat16),
            jax.ShapeDtypeStruct((2, ROWS, D), jnp.bfloat16),
            jax.ShapeDtypeStruct((ROWS // 2, fw.shape[1]), jnp.float32),
        )
        out_specs = (vmem, hbm, vmem)
        scratch.append(pltpu.VMEM((ROWS, D), jnp.bfloat16))
    else:
        outs = (jax.ShapeDtypeStruct((ROWS, D), jnp.bfloat16),) * 2
        out_specs = (vmem, hbm)
    return pl.pallas_call(
        lambda *refs: layer_kernel(final, req, *refs),
        name="last_layer" if final else "first_layer",
        out_shape=outs,
        in_specs=specs,
        out_specs=out_specs,
        scratch_shapes=scratch,
        input_output_aliases=aliases,
        compiler_params=pltpu.CompilerParams(vmem_limit_bytes=56 << 20),
    )(*operands)


def on_device(
    hidden,
    text_kv,
    stale_kv,
    modulation,
    score_gain,
    qkv_weight,
    out_weight,
    final_mod,
    final_weight,
    latent,
    step_index,
):
    section = lax.axis_index("section")
    shard = lax.axis_index("shard")
    z_hi, x_at, core = shard // 8, (shard // 2) % 4, shard % 2

    qkv = qkv_weight[0]
    half_kv = qkv[:, HW:]
    half_oq = jnp.concatenate([qkv[:, :HW], out_weight[0].T], 1)
    keep = jnp.where(core == 0, half_kv, half_oq)
    got = core_flip(jnp.where(core == 0, half_oq, half_kv))
    mine_block = jnp.concatenate(
        [jnp.where(core == 0, keep, got), jnp.where(core == 0, got, keep)], 0
    )
    near_z, near_x = mine_block[:, :ZC], mine_block[:, ZC:]
    text = jnp.pad(text_kv[0], ((0, 0), (0, TXT_PAD - TXT), (0, 0)))

    before_x, after_x = x_shift(near_x, 1), x_shift(near_x, -1)
    opposite_z = z_flip(near_z)
    before_y, after_y = y_shift(stale_kv[0], 1), y_shift(stale_kv[0], -1)
    far_x = x_relay(jnp.where(core == 0, after(before_x, text), after_x))
    three_x = jnp.concatenate([near_x, before_x, after_x], 0)
    opposite_three = z_flip(three_x)
    pair_z = jnp.concatenate([near_z, opposite_z], 0)
    before_z, after_z = x_shift(pair_z, 1), x_shift(pair_z, -1)
    far_y = y_relay(jnp.where(core == 0, after(before_y, far_x), after_y))
    far_z = x_relay(jnp.where(core == 0, before_z, after_z))
    opposite_far = z_flip(after(far_x, opposite_three))
    early = (near_z, opposite_z, three_x, far_x)
    their_early = tuple(core_flip(after(piece, before_z)) for piece in early)
    their_before_z = core_flip(after(before_z, far_y))
    their_after_z = core_flip(after(after_z, far_y))
    their_far_z = core_flip(after(far_z, far_y))
    their_opposite_three = core_flip(after(opposite_three, far_y))
    their_opposite_far = core_flip(after(opposite_far, far_y))
    mine = (*early, before_z, after_z, far_z, opposite_three, opposite_far)
    theirs = (*their_early, their_before_z, their_after_z, their_far_z,
              their_opposite_three, their_opposite_far)
    stale = (before_y, after_y, far_y)
    gain = jnp.tile(score_gain[0] * (1.0 / math.sqrt(HEAD)), WIDE // HEAD)[None, :]
    rows = [
        ((z_hi ^ slot) * 4 + (x_at + dx) % 4) * BLK for slot in range(2) for dx in (0, 3, 1, 2)
    ]
    scalars = jnp.stack([core, *rows, section]).astype(jnp.int32)

    def layer(x, r, last=None):
        return run_layer(
            scalars, x, modulation[0], gain, mine, theirs, stale, text, r, last
        )

    fresh_first, arrived = [], []
    for r in range(2):
        x_next, fresh = layer(hidden, r)
        fresh_first.append(fresh)
        arrived.append(lax.ppermute(x_next, "section", [(0, 1)]))
    velocity, new_kv = [], None
    for r in range(2):
        low, new_kv, high = layer(arrived[r], r, (final_mod, final_weight, fresh_first[r], new_kv))
        sent = lax.ppermute(low, "section", [(1, 0)])
        velocity.append(jnp.where(section == 0, sent.astype(jnp.float32), high))
    velocity_mine = jnp.stack(velocity)
    sig = sigma_of(step_index)[:, None, None]
    sig_next = sigma_of(step_index + 1)[:, None, None]
    latent_next = latent + (sig_next - sig) * velocity_mine
    denoised = latent - sig * velocity_mine
    return (new_kv[None], latent_next, denoised)


def solution(mesh):
    in_specs = (
        P("shard", "patch", None),
        P("section", "shard", None, None),
        P("section", "shard", "patch", None),
        P("section", "shard", None, None),
        P("section", None),
        P("section", "shard", None),
        P("section", None, "shard"),
        P("shard", None, None),
        P(),
        P("shard", ("patch", "section"), None),
        P("shard"),
    )
    out_specs = (
        P("section", "shard", "patch", None),
        P("shard", ("patch", "section"), None),
        P("shard", ("patch", "section"), None),
    )
    return jax.shard_map(
        on_device, mesh=mesh, in_specs=in_specs, out_specs=out_specs, check_vma=False
    )
```

```python
import math

import jax
import jax.numpy as jnp
from jax import lax
from jax.experimental import pallas as pl
from jax.experimental.pallas import tpu as pltpu
from jax.sharding import PartitionSpec as P

HEAD = 64
NSTEPS = 28
D = 2432
HW = 1216
ROWS = 256
TXT = 154
TXT_PAD = 160
KEYS = 4 * ROWS + TXT_PAD
BLK = 304
ZC = 1408
XC = D - ZC
WIDE = 1280
LANE = 128
NT = 256

eps_norm = 1e-06
flow_shift = 3.0


def sigma_of(step):
    s = 1.0 - step.astype(jnp.float32) / NSTEPS
    return flow_shift * s / (1.0 + (flow_shift - 1.0) * s)


def shard_pairs(flip_z=0, flip_core=0):
    return [(i, i ^ (8 * flip_z) ^ flip_core) for i in range(16)]


def z_flip(value):
    return lax.ppermute(value, "shard", shard_pairs(flip_z=1))


def core_flip(value):
    return lax.ppermute(value, "shard", shard_pairs(flip_core=1))


def x_turn(value, step):
    pairs = []
    for z in range(2):
        for x in range(4):
            for c in range(2):
                dx = step if c == 0 else -step
                pairs.append((z * 8 + x * 2 + c, z * 8 + ((x + dx) % 4) * 2 + c))
    return lax.ppermute(value, "shard", pairs)


def y_turn(value, step):
    pairs = []
    for y in range(4):
        for k in range(16):
            dy = step if k % 2 == 0 else -step
            pairs.append((y * 16 + k, ((y + dy) % 4) * 16 + k))
    return lax.ppermute(value, ("patch", "shard"), pairs)


def after(value, *earlier):
    return lax.optimization_barrier((value, *earlier))[0]


def group_scale(p, ones_ref):
    total = jnp.dot(
        (p * p).astype(jnp.bfloat16), ones_ref[...], preferred_element_type=jnp.float32
    )
    return lax.rsqrt(total * (1.0 / HEAD) + eps_norm)


def norm_rows(src_ref, shift_ref, scale_ref, dst_ref):
    step = 32

    def body(i, _):
        r = pl.multiple_of(i * step, step)
        xf = src_ref[pl.ds(r, step), :].astype(jnp.float32)
        mean = jnp.mean(xf, -1, keepdims=True)
        cent = xf - mean
        var = jnp.mean(cent * cent, -1, keepdims=True)
        out = cent * lax.rsqrt(var + eps_norm) * (1.0 + scale_ref[...]) + shift_ref[...]
        dst_ref[pl.ds(r, step), :] = out.astype(jnp.bfloat16)
        return 0

    lax.fori_loop(0, ROWS // step, body, 0)


def layer_kernel(final, req, *refs):
    sc, x_hbm, mod_ref, gain_ref = refs[:4]
    mine = refs[4:11]
    theirs = refs[11:18]
    stale = refs[18:21]
    text_ref = refs[21]
    refs = refs[22:]
    mod_ref = mod_ref.at[req]
    if final:
        fmod_ref, fw_ref, early_ref = refs[0].at[req], refs[1], refs[2]
        refs = refs[4:] if req else refs[3:]
        low_ref, fresh_ref, high_ref = refs[:3]
        fresh_ref = fresh_ref.at[req]
        w_kv, w_q, w_o, kv, normed, qbuf, attn, ones, x_ref, sems, x_out = refs[3:]
    else:
        x_hbm = x_hbm.at[req]
        x_out, fresh_ref = refs[:2]
        w_kv, w_q, w_o, kv, normed, qbuf, attn, ones, x_ref, sems = refs[2:]
    row_of = lambda slot, j: pl.multiple_of(sc[1 + slot * 4 + j], 16)

    def put(ref, at, col, count, dst, slot, j, dst_col, sem):
        pltpu.make_async_copy(
            ref.at[pl.ds(at, BLK), pl.ds(col, count)],
            dst.at[pl.ds(row_of(slot, j), BLK), pl.ds(dst_col, count)],
            sem,
        ).start()

    kv_order, oq_order = (0, 1, 2, 3), (0, 2, 1, 3)

    def spread_z(pieces, order, col, count, dst, dst_col, sem):
        for j, ref in zip(order, pieces[:4]):
            for slot in range(2):
                put(ref, slot * BLK, col, count, dst, slot, j, dst_col, sem)

    def spread_x(pieces, order, dst, dst_col, sem):
        four, three, far = pieces[4:]
        for i in range(4):
            put(four, i * BLK, 0, XC, dst, 0, order[i], dst_col, sem)
        for i in range(3):
            put(three, i * BLK, 0, XC, dst, 1, order[i], dst_col, sem)
        put(far, 0, 0, XC, dst, 1, 3, dst_col, sem)

    def by_core(step):
        @pl.when(sc[0] == 0)
        def _():
            step(mine, theirs)

        @pl.when(sc[0] != 0)
        def _():
            step(theirs, mine)

    def fetch_kv_z(kv_pieces, oq_pieces):
        spread_z(kv_pieces, kv_order, 0, ZC, w_kv, 0, sems.at[0])

    def fetch_kv_x(kv_pieces, oq_pieces):
        spread_x(kv_pieces, kv_order, w_kv, ZC, sems.at[1])

    def fetch_q(kv_pieces, oq_pieces):
        spread_z(oq_pieces, oq_order, 0, WIDE, w_q, 0, sems.at[2])

    def fetch_out(kv_pieces, oq_pieces):
        spread_z(oq_pieces, oq_order, D - WIDE, ZC + WIDE - D, w_o, 0, sems.at[4])
        spread_x(oq_pieces, oq_order, w_o, ZC + WIDE - D, sems.at[4])

    def fetch_keys():
        for j, ref in enumerate((*stale, text_ref)):
            count = ROWS if j < 3 else TXT_PAD
            pltpu.make_async_copy(
                ref.at[req], kv.at[pl.ds((j + 1) * ROWS, count), :], sems.at[3]
            ).start()

    def wait(dst, sem):
        pltpu.make_async_copy(dst, dst, sem).wait()

    pltpu.make_async_copy(x_hbm, x_ref, sems.at[5]).start()
    by_core(fetch_kv_z)
    wait(x_ref, sems.at[5])

    norm_rows(x_ref, mod_ref.at[0:1, :], mod_ref.at[1:2, :], normed)
    gi = lax.broadcasted_iota(jnp.int32, (NT, NT), 0) // HEAD
    gj = lax.broadcasted_iota(jnp.int32, (NT, NT), 1) // HEAD
    ones[...] = jnp.where(gi == gj, 1.0, 0.0).astype(jnp.bfloat16)

    by_core(fetch_kv_x)
    wait(w_kv.at[:, pl.ds(0, ZC)], sems.at[0])
    by_core(fetch_q)

    def key_block(j, _):
        c = pl.multiple_of(j * NT, NT)
        p = jnp.dot(normed[...], w_kv[:, pl.ds(c, NT)], preferred_element_type=jnp.float32)
        col = lax.broadcasted_iota(jnp.int32, (ROWS, NT), 1) + c
        out = p * jnp.where(col < HW, group_scale(p, ones), 1.0)
        kv[pl.ds(0, ROWS), pl.ds(c, NT)] = out.astype(jnp.bfloat16)
        return 0

    lax.fori_loop(0, WIDE // NT, key_block, 0)
    wait(w_kv.at[:, pl.ds(ZC, XC)], sems.at[1])
    fetch_keys()
    vw = 384

    def value_block(j, _):
        c = pl.multiple_of(WIDE + j * vw, LANE)
        p = jnp.dot(normed[...], w_kv[:, pl.ds(c, vw)], preferred_element_type=jnp.float32)
        kv[pl.ds(0, ROWS), pl.ds(c, vw)] = p.astype(jnp.bfloat16)
        return 0

    lax.fori_loop(0, (D - WIDE) // vw, value_block, 0)
    new_rows = kv.at[pl.ds(0, ROWS), :]
    spare = w_kv.at[pl.ds(0, ROWS), :]
    if final:

        @pl.when(sc[9] == 0)
        def _():
            pltpu.make_async_copy(early_ref, spare, sems.at[6]).start()

    else:
        pltpu.make_async_copy(new_rows, fresh_ref, sems.at[6]).start()
    wait(w_q, sems.at[2])
    by_core(fetch_out)

    def query_block(j, _):
        c = pl.multiple_of(j * NT, NT)
        p = jnp.dot(normed[...], w_q[:, pl.ds(c, NT)], preferred_element_type=jnp.float32)
        q = p * group_scale(p, ones) * gain_ref[:, pl.ds(c, NT)]
        qbuf[:, pl.ds(c, NT)] = q.astype(jnp.bfloat16)
        return 0

    lax.fori_loop(0, WIDE // NT, query_block, 0)
    wait(kv.at[pl.ds(ROWS, KEYS - ROWS), :], sems.at[3])

    low = lax.broadcasted_iota(jnp.int32, (ROWS, LANE), 1) < HEAD
    zero = jnp.zeros((ROWS, LANE), jnp.bfloat16)
    chunks = [(i * ROWS, ROWS) for i in range(4)] + [(4 * ROWS, TXT_PAD)]
    contract = (((1,), (1,)), ((), ()))
    one_rows = jnp.ones((ROWS, LANE), jnp.bfloat16)
    text_rows = jnp.where(
        lax.broadcasted_iota(jnp.int32, (TXT_PAD, LANE), 0) < TXT, 1.0, 0.0
    ).astype(jnp.bfloat16)

    def attend(q, key_of, vc):
        acc = None
        for start, count in chunks:
            v = kv[pl.ds(start, count), pl.ds(vc, LANE)]
            s = lax.dot_general(
                q, key_of(start, count), contract, preferred_element_type=jnp.float32
            )
            w = jnp.exp(s).astype(jnp.bfloat16)
            v_one = jnp.concatenate([v, one_rows if count == ROWS else text_rows], 1)
            part = jnp.dot(w, v_one, preferred_element_type=jnp.float32)
            acc = part if acc is None else acc + part
        return acc[:, :LANE] / acc[:, LANE:]

    def pair(j, _):
        c = pl.multiple_of(j * LANE, LANE)
        n = pl.multiple_of(c + LANE, LANE)
        q_c, q_n = qbuf[:, pl.ds(c, LANE)], qbuf[:, pl.ds(n, LANE)]
        q = jnp.concatenate([jnp.where(low, zero, q_c), jnp.where(low, q_n, zero)], 0)

        def key_of(start, count):
            return jnp.where(
                low[:count], kv[pl.ds(start, count), pl.ds(n, LANE)],
                kv[pl.ds(start, count), pl.ds(c, LANE)],
            )

        out = attend(q, key_of, pl.multiple_of(c + 10 * LANE, LANE))
        out = jnp.where(low, out[:ROWS], out[ROWS:])
        attn[:, pl.ds(n, LANE)] = out.astype(jnp.bfloat16)
        return 0

    lax.fori_loop(0, 9, pair, 0, unroll=3)
    first = attend(
        jnp.where(low, qbuf[:, pl.ds(0, LANE)], zero),
        lambda start, count: kv[pl.ds(start, count), pl.ds(0, LANE)],
        9 * LANE,
    )
    attn[:, pl.ds(0, LANE)] = jnp.where(low, 0.0, first).astype(jnp.bfloat16)

    if final:

        @pl.when(sc[9] == 0)
        def _():
            wait(spare, sems.at[6])
            pltpu.make_async_copy(spare, fresh_ref, sems.at[6]).start()

        @pl.when(sc[9] != 0)
        def _():
            pltpu.make_async_copy(new_rows, fresh_ref, sems.at[6]).start()

    wait(w_o, sems.at[4])

    def out_block(c, width):
        proj = lax.dot_general(
            attn[...], w_o[pl.ds(c, width), :], contract, preferred_element_type=jnp.float32
        )
        xf = x_ref[:, pl.ds(c, width)].astype(jnp.float32)
        gate = mod_ref[2:3, pl.ds(c, width)]
        x_out[:, pl.ds(c, width)] = (xf + gate * proj).astype(jnp.bfloat16)

    def out_body(j, _):
        out_block(pl.multiple_of(j * NT, NT), NT)
        return 0

    lax.fori_loop(0, D // NT, out_body, 0)
    out_block((D // NT) * NT, D % NT)
    if final:
        norm_rows(x_out, fmod_ref.at[0:1, :], fmod_ref.at[1:2, :], normed)
        vel = jnp.dot(normed[...], fw_ref[...], preferred_element_type=jnp.float32)
        half = ROWS // 2
        low_ref[...] = vel[:half].astype(jnp.bfloat16)
        high_ref[...] = vel[half:]
    wait(new_rows, sems.at[6])


def run_layer(scalars, x, mod, gain, mine, theirs, stale, text, req, last=None):
    vmem = pl.BlockSpec(memory_space=pltpu.VMEM)
    hbm = pl.BlockSpec(memory_space=pl.ANY)
    final = last is not None
    operands = [scalars, x, mod, gain, *mine, *theirs, *stale, text]
    specs = [pl.BlockSpec(memory_space=pltpu.SMEM), hbm, vmem, vmem] + [hbm] * 18
    scratch = [
        pltpu.VMEM((D, D), jnp.bfloat16),
        pltpu.VMEM((D, WIDE), jnp.bfloat16),
        pltpu.VMEM((D, WIDE), jnp.bfloat16),
        pltpu.VMEM((KEYS, D), jnp.bfloat16),
        pltpu.VMEM((ROWS, D), jnp.bfloat16),
        pltpu.VMEM((ROWS, WIDE), jnp.bfloat16),
        pltpu.VMEM((ROWS, WIDE), jnp.bfloat16),
        pltpu.VMEM((NT, NT), jnp.bfloat16),
        pltpu.VMEM((ROWS, D), jnp.bfloat16),
        pltpu.SemaphoreType.DMA((7,)),
    ]
    aliases = {}
    if final:
        fmod, fw, early, new_kv = last
        operands += [fmod, fw, early]
        specs += [vmem, vmem, hbm]
        if req:
            aliases = {len(operands): 1}
            operands.append(new_kv)
            specs.append(hbm)
        outs = (
            jax.ShapeDtypeStruct((ROWS // 2, fw.shape[1]), jnp.bfloat16),
            jax.ShapeDtypeStruct((2, ROWS, D), jnp.bfloat16),
            jax.ShapeDtypeStruct((ROWS // 2, fw.shape[1]), jnp.float32),
        )
        out_specs = (vmem, hbm, vmem)
        scratch.append(pltpu.VMEM((ROWS, D), jnp.bfloat16))
    else:
        outs = (jax.ShapeDtypeStruct((ROWS, D), jnp.bfloat16),) * 2
        out_specs = (vmem, hbm)
    return pl.pallas_call(
        lambda *refs: layer_kernel(final, req, *refs),
        name="last_layer" if final else "first_layer",
        out_shape=outs,
        in_specs=specs,
        out_specs=out_specs,
        scratch_shapes=scratch,
        input_output_aliases=aliases,
        compiler_params=pltpu.CompilerParams(vmem_limit_bytes=56 << 20),
    )(*operands)


def on_device(
    hidden,
    text_kv,
    stale_kv,
    modulation,
    score_gain,
    qkv_weight,
    out_weight,
    final_mod,
    final_weight,
    latent,
    step_index,
):
    section = lax.axis_index("section")
    shard = lax.axis_index("shard")
    z_hi, x_at, core = shard // 8, (shard // 2) % 4, shard % 2

    qkv = qkv_weight[0]
    half_kv = qkv[:, HW:]
    half_oq = jnp.concatenate([qkv[:, :HW], out_weight[0].T], 1)
    keep = jnp.where(core == 0, half_kv, half_oq)
    got = core_flip(jnp.where(core == 0, half_oq, half_kv))
    mine_block = jnp.concatenate(
        [jnp.where(core == 0, keep, got), jnp.where(core == 0, got, keep)], 0
    )
    near_z, near_x = mine_block[:, :ZC], mine_block[:, ZC:]
    text = jnp.pad(text_kv[0], ((0, 0), (0, TXT_PAD - TXT), (0, 0)))

    one_x = x_turn(near_x, 1)
    opposite_z = z_flip(near_z)
    one_y = y_turn(stale_kv[0], 1)
    two_x = x_turn(near_x, -1)
    far_x = x_turn(after(one_x, text), 1)
    two_y = y_turn(after(stale_kv[0], one_y), -1)
    far_y = y_turn(one_y, 1)
    three_x = jnp.concatenate([near_x, one_x, two_x], 0)
    opposite_three = z_flip(three_x)
    pair_z = jnp.concatenate([near_z, opposite_z], 0)
    one_z, two_z = x_turn(pair_z, 1), x_turn(pair_z, -1)
    far_z = x_turn(one_z, 1)
    opposite_far = z_flip(after(far_x, opposite_three))
    four_x = jnp.concatenate([three_x, far_x], 0)
    their_pair = core_flip(after(pair_z, far_x))
    their_four_x = core_flip(after(four_x, far_x))
    their_one_z = core_flip(after(one_z, two_y))
    their_two_z = core_flip(after(two_z, two_y))
    their_far_z = core_flip(after(far_z, far_y))
    their_opposite_three = core_flip(after(opposite_three, far_y))
    their_opposite_far = core_flip(after(opposite_far, far_y))
    mine = (pair_z, one_z, two_z, far_z, four_x, opposite_three, opposite_far)
    theirs = (their_pair, their_one_z, their_two_z, their_far_z,
              their_four_x, their_opposite_three, their_opposite_far)
    stale = (one_y, two_y, far_y)
    gain = jnp.tile(score_gain[0] * (1.0 / math.sqrt(HEAD)), WIDE // HEAD)[None, :]
    rows = [
        ((z_hi ^ slot) * 4 + (x_at + dx) % 4) * BLK for slot in range(2) for dx in (0, 3, 1, 2)
    ]
    scalars = jnp.stack([core, *rows, section]).astype(jnp.int32)

    def layer(x, r, last=None):
        return run_layer(
            scalars, x, modulation[0], gain, mine, theirs, stale, text, r, last
        )

    fresh_first, arrived = [], []
    for r in range(2):
        x_next, fresh = layer(hidden, r)
        fresh_first.append(fresh)
        arrived.append(lax.ppermute(x_next, "section", [(0, 1)]))
    velocity, new_kv = [], None
    for r in range(2):
        low, new_kv, high = layer(arrived[r], r, (final_mod, final_weight, fresh_first[r], new_kv))
        sent = lax.ppermute(low, "section", [(1, 0)])
        velocity.append(jnp.where(section == 0, sent.astype(jnp.float32), high))
    velocity_mine = jnp.stack(velocity)
    sig = sigma_of(step_index)[:, None, None]
    sig_next = sigma_of(step_index + 1)[:, None, None]
    latent_next = latent + (sig_next - sig) * velocity_mine
    denoised = latent - sig * velocity_mine
    return (new_kv[None], latent_next, denoised)


def solution(mesh):
    in_specs = (
        P("shard", "patch", None),
        P("section", "shard", None, None),
        P("section", "shard", "patch", None),
        P("section", "shard", None, None),
        P("section", None),
        P("section", "shard", None),
        P("section", None, "shard"),
        P("shard", None, None),
        P(),
        P("shard", ("patch", "section"), None),
        P("shard"),
    )
    out_specs = (
        P("section", "shard", "patch", None),
        P("shard", ("patch", "section"), None),
        P("shard", ("patch", "section"), None),
    )
    return jax.shard_map(
        on_device, mesh=mesh, in_specs=in_specs, out_specs=out_specs, check_vma=False
    )
```

```python
import math

import jax
import jax.numpy as jnp
from jax import lax
from jax.experimental import pallas as pl
from jax.experimental.pallas import tpu as pltpu
from jax.sharding import PartitionSpec as P

HEAD = 64
NSTEPS = 28
D = 2432
HW = 1216
ROWS = 256
TXT = 154
TXT_PAD = 160
KEYS = 4 * ROWS + TXT_PAD
BLK = 304
ZC = 1408
XC = D - ZC
WIDE = 1280
LANE = 128
NT = 256

eps_norm = 1e-06
flow_shift = 3.0


def sigma_of(step):
    s = 1.0 - step.astype(jnp.float32) / NSTEPS
    return flow_shift * s / (1.0 + (flow_shift - 1.0) * s)


def shard_pairs(flip_z=0, dx=0, flip_core=0):
    pairs = []
    for z in range(2):
        for x in range(4):
            for c in range(2):
                src = z * 8 + x * 2 + c
                dst = (z ^ flip_z) * 8 + ((x + dx) % 4) * 2 + (c ^ flip_core)
                pairs.append((src, dst))
    return pairs


def ring_pairs(step):
    return [(i, (i + step) % 4) for i in range(4)]


def x_shift(value, dx):
    return lax.ppermute(value, "shard", shard_pairs(dx=dx))


def z_flip(value):
    return lax.ppermute(value, "shard", shard_pairs(flip_z=1))


def core_flip(value):
    return lax.ppermute(value, "shard", shard_pairs(flip_core=1))


def y_shift(value, dy):
    return lax.ppermute(value, "patch", ring_pairs(dy))


def x_relay(value):
    pairs = []
    for z in range(2):
        for x in range(4):
            for c in range(2):
                dx = 1 if c == 0 else -1
                pairs.append((z * 8 + x * 2 + c, z * 8 + ((x + dx) % 4) * 2 + c))
    return lax.ppermute(value, "shard", pairs)


def y_relay(value):
    pairs = []
    for y in range(4):
        for k in range(16):
            dy = 1 if k % 2 == 0 else -1
            pairs.append((y * 16 + k, ((y + dy) % 4) * 16 + k))
    return lax.ppermute(value, ("patch", "shard"), pairs)


def after(value, *earlier):
    return lax.optimization_barrier((value, *earlier))[0]


def group_scale(p, ones_ref):
    total = jnp.dot(
        (p * p).astype(jnp.bfloat16), ones_ref[...], preferred_element_type=jnp.float32
    )
    return lax.rsqrt(total * (1.0 / HEAD) + eps_norm)


def norm_rows(src_ref, shift_ref, scale_ref, dst_ref):
    step = 32

    def body(i, _):
        r = pl.multiple_of(i * step, step)
        xf = src_ref[pl.ds(r, step), :].astype(jnp.float32)
        mean = jnp.mean(xf, -1, keepdims=True)
        cent = xf - mean
        var = jnp.mean(cent * cent, -1, keepdims=True)
        out = cent * lax.rsqrt(var + eps_norm) * (1.0 + scale_ref[...]) + shift_ref[...]
        dst_ref[pl.ds(r, step), :] = out.astype(jnp.bfloat16)
        return 0

    lax.fori_loop(0, ROWS // step, body, 0)


def layer_kernel(final, req, *refs):
    sc, x_hbm, mod_ref, gain_ref = refs[:4]
    mine = refs[4:11]
    theirs = refs[11:18]
    stale = refs[18:21]
    text_ref = refs[21]
    refs = refs[22:]
    mod_ref = mod_ref.at[req]
    if final:
        fmod_ref, fw_ref, early_ref = refs[0].at[req], refs[1], refs[2]
        refs = refs[4:] if req else refs[3:]
        low_ref, fresh_ref, high_ref = refs[:3]
        fresh_ref = fresh_ref.at[req]
        w_kv, w_q, w_o, kv, normed, qbuf, attn, ones, x_ref, sems, x_out = refs[3:]
    else:
        x_hbm = x_hbm.at[req]
        x_out, fresh_ref = refs[:2]
        w_kv, w_q, w_o, kv, normed, qbuf, attn, ones, x_ref, sems = refs[2:]
    row_of = lambda slot, j: pl.multiple_of(sc[1 + slot * 4 + j], 16)

    def put(ref, at, col, count, dst, slot, j, dst_col, sem):
        pltpu.make_async_copy(
            ref.at[pl.ds(at, BLK), pl.ds(col, count)],
            dst.at[pl.ds(row_of(slot, j), BLK), pl.ds(dst_col, count)],
            sem,
        ).start()

    def spread_z(pieces, col, count, dst, dst_col, sem):
        for j, ref in enumerate(pieces[:4]):
            for slot in range(2):
                put(ref, slot * BLK, col, count, dst, slot, j, dst_col, sem)

    def spread_x(pieces, dst, dst_col, sem):
        four, three, far = pieces[4:]
        for j in range(4):
            put(four, j * BLK, 0, XC, dst, 0, j, dst_col, sem)
        for j in range(3):
            put(three, j * BLK, 0, XC, dst, 1, j, dst_col, sem)
        put(far, 0, 0, XC, dst, 1, 3, dst_col, sem)

    def by_core(step):
        @pl.when(sc[0] == 0)
        def _():
            step(mine, theirs)

        @pl.when(sc[0] != 0)
        def _():
            step(theirs, mine)

    def fetch_kv_z(kv_pieces, oq_pieces):
        spread_z(kv_pieces, 0, ZC, w_kv, 0, sems.at[0])

    def fetch_kv_x(kv_pieces, oq_pieces):
        spread_x(kv_pieces, w_kv, ZC, sems.at[1])

    def fetch_q(kv_pieces, oq_pieces):
        spread_z(oq_pieces, 0, WIDE, w_q, 0, sems.at[2])

    def fetch_out(kv_pieces, oq_pieces):
        spread_z(oq_pieces, D - WIDE, ZC + WIDE - D, w_o, 0, sems.at[4])
        spread_x(oq_pieces, w_o, ZC + WIDE - D, sems.at[4])

    def fetch_keys():
        for j, ref in enumerate((*stale, text_ref)):
            count = ROWS if j < 3 else TXT_PAD
            pltpu.make_async_copy(
                ref.at[req], kv.at[pl.ds((j + 1) * ROWS, count), :], sems.at[3]
            ).start()

    def wait(dst, sem):
        pltpu.make_async_copy(dst, dst, sem).wait()

    pltpu.make_async_copy(x_hbm, x_ref, sems.at[5]).start()
    by_core(fetch_kv_z)
    wait(x_ref, sems.at[5])

    norm_rows(x_ref, mod_ref.at[0:1, :], mod_ref.at[1:2, :], normed)
    gi = lax.broadcasted_iota(jnp.int32, (NT, NT), 0) // HEAD
    gj = lax.broadcasted_iota(jnp.int32, (NT, NT), 1) // HEAD
    ones[...] = jnp.where(gi == gj, 1.0, 0.0).astype(jnp.bfloat16)

    by_core(fetch_kv_x)
    wait(w_kv.at[:, pl.ds(0, ZC)], sems.at[0])
    by_core(fetch_q)

    def key_block(j, _):
        c = pl.multiple_of(j * NT, NT)
        p = jnp.dot(normed[...], w_kv[:, pl.ds(c, NT)], preferred_element_type=jnp.float32)
        col = lax.broadcasted_iota(jnp.int32, (ROWS, NT), 1) + c
        out = p * jnp.where(col < HW, group_scale(p, ones), 1.0)
        kv[pl.ds(0, ROWS), pl.ds(c, NT)] = out.astype(jnp.bfloat16)
        return 0

    lax.fori_loop(0, WIDE // NT, key_block, 0)
    wait(w_kv.at[:, pl.ds(ZC, XC)], sems.at[1])
    fetch_keys()
    vw = 384

    def value_block(j, _):
        c = pl.multiple_of(WIDE + j * vw, LANE)
        p = jnp.dot(normed[...], w_kv[:, pl.ds(c, vw)], preferred_element_type=jnp.float32)
        kv[pl.ds(0, ROWS), pl.ds(c, vw)] = p.astype(jnp.bfloat16)
        return 0

    lax.fori_loop(0, (D - WIDE) // vw, value_block, 0)
    new_rows = kv.at[pl.ds(0, ROWS), :]
    spare = w_kv.at[pl.ds(0, ROWS), :]
    if final:

        @pl.when(sc[9] == 0)
        def _():
            pltpu.make_async_copy(early_ref, spare, sems.at[6]).start()

    else:
        pltpu.make_async_copy(new_rows, fresh_ref, sems.at[6]).start()
    wait(w_q, sems.at[2])
    by_core(fetch_out)

    def query_block(j, _):
        c = pl.multiple_of(j * NT, NT)
        p = jnp.dot(normed[...], w_q[:, pl.ds(c, NT)], preferred_element_type=jnp.float32)
        q = p * group_scale(p, ones) * gain_ref[:, pl.ds(c, NT)]
        qbuf[:, pl.ds(c, NT)] = q.astype(jnp.bfloat16)
        return 0

    lax.fori_loop(0, WIDE // NT, query_block, 0)
    wait(kv.at[pl.ds(ROWS, KEYS - ROWS), :], sems.at[3])

    low = lax.broadcasted_iota(jnp.int32, (ROWS, LANE), 1) < HEAD
    zero = jnp.zeros((ROWS, LANE), jnp.bfloat16)
    chunks = [(i * ROWS, ROWS) for i in range(4)] + [(4 * ROWS, TXT_PAD)]
    contract = (((1,), (1,)), ((), ()))
    one_rows = jnp.ones((ROWS, LANE), jnp.bfloat16)
    text_rows = jnp.where(
        lax.broadcasted_iota(jnp.int32, (TXT_PAD, LANE), 0) < TXT, 1.0, 0.0
    ).astype(jnp.bfloat16)

    def attend(q, key_of, vc):
        acc = None
        for start, count in chunks:
            v = kv[pl.ds(start, count), pl.ds(vc, LANE)]
            s = lax.dot_general(
                q, key_of(start, count), contract, preferred_element_type=jnp.float32
            )
            w = jnp.exp(s).astype(jnp.bfloat16)
            v_one = jnp.concatenate([v, one_rows if count == ROWS else text_rows], 1)
            part = jnp.dot(w, v_one, preferred_element_type=jnp.float32)
            acc = part if acc is None else acc + part
        return acc[:, :LANE] / acc[:, LANE:]

    def pair(j, _):
        c = pl.multiple_of(j * LANE, LANE)
        n = pl.multiple_of(c + LANE, LANE)
        q_c, q_n = qbuf[:, pl.ds(c, LANE)], qbuf[:, pl.ds(n, LANE)]
        q = jnp.concatenate([jnp.where(low, zero, q_c), jnp.where(low, q_n, zero)], 0)

        def key_of(start, count):
            return jnp.where(
                low[:count], kv[pl.ds(start, count), pl.ds(n, LANE)],
                kv[pl.ds(start, count), pl.ds(c, LANE)],
            )

        out = attend(q, key_of, pl.multiple_of(c + 10 * LANE, LANE))
        out = jnp.where(low, out[:ROWS], out[ROWS:])
        attn[:, pl.ds(n, LANE)] = out.astype(jnp.bfloat16)
        return 0

    lax.fori_loop(0, 9, pair, 0, unroll=3)
    first = attend(
        jnp.where(low, qbuf[:, pl.ds(0, LANE)], zero),
        lambda start, count: kv[pl.ds(start, count), pl.ds(0, LANE)],
        9 * LANE,
    )
    attn[:, pl.ds(0, LANE)] = jnp.where(low, 0.0, first).astype(jnp.bfloat16)

    if final:

        @pl.when(sc[9] == 0)
        def _():
            wait(spare, sems.at[6])
            pltpu.make_async_copy(spare, fresh_ref, sems.at[6]).start()

        @pl.when(sc[9] != 0)
        def _():
            pltpu.make_async_copy(new_rows, fresh_ref, sems.at[6]).start()

    wait(w_o, sems.at[4])

    def out_block(c, width):
        proj = lax.dot_general(
            attn[...], w_o[pl.ds(c, width), :], contract, preferred_element_type=jnp.float32
        )
        xf = x_ref[:, pl.ds(c, width)].astype(jnp.float32)
        gate = mod_ref[2:3, pl.ds(c, width)]
        x_out[:, pl.ds(c, width)] = (xf + gate * proj).astype(jnp.bfloat16)

    def out_body(j, _):
        out_block(pl.multiple_of(j * NT, NT), NT)
        return 0

    lax.fori_loop(0, D // NT, out_body, 0)
    out_block((D // NT) * NT, D % NT)
    if final:
        norm_rows(x_out, fmod_ref.at[0:1, :], fmod_ref.at[1:2, :], normed)
        vel = jnp.dot(normed[...], fw_ref[...], preferred_element_type=jnp.float32)
        half = ROWS // 2
        low_ref[...] = vel[:half].astype(jnp.bfloat16)
        high_ref[...] = vel[half:]
    wait(new_rows, sems.at[6])


def run_layer(scalars, x, mod, gain, mine, theirs, stale, text, req, last=None):
    vmem = pl.BlockSpec(memory_space=pltpu.VMEM)
    hbm = pl.BlockSpec(memory_space=pl.ANY)
    final = last is not None
    operands = [scalars, x, mod, gain, *mine, *theirs, *stale, text]
    specs = [pl.BlockSpec(memory_space=pltpu.SMEM), hbm, vmem, vmem] + [hbm] * 18
    scratch = [
        pltpu.VMEM((D, D), jnp.bfloat16),
        pltpu.VMEM((D, WIDE), jnp.bfloat16),
        pltpu.VMEM((D, WIDE), jnp.bfloat16),
        pltpu.VMEM((KEYS, D), jnp.bfloat16),
        pltpu.VMEM((ROWS, D), jnp.bfloat16),
        pltpu.VMEM((ROWS, WIDE), jnp.bfloat16),
        pltpu.VMEM((ROWS, WIDE), jnp.bfloat16),
        pltpu.VMEM((NT, NT), jnp.bfloat16),
        pltpu.VMEM((ROWS, D), jnp.bfloat16),
        pltpu.SemaphoreType.DMA((7,)),
    ]
    aliases = {}
    if final:
        fmod, fw, early, new_kv = last
        operands += [fmod, fw, early]
        specs += [vmem, vmem, hbm]
        if req:
            aliases = {len(operands): 1}
            operands.append(new_kv)
            specs.append(hbm)
        outs = (
            jax.ShapeDtypeStruct((ROWS // 2, fw.shape[1]), jnp.bfloat16),
            jax.ShapeDtypeStruct((2, ROWS, D), jnp.bfloat16),
            jax.ShapeDtypeStruct((ROWS // 2, fw.shape[1]), jnp.float32),
        )
        out_specs = (vmem, hbm, vmem)
        scratch.append(pltpu.VMEM((ROWS, D), jnp.bfloat16))
    else:
        outs = (jax.ShapeDtypeStruct((ROWS, D), jnp.bfloat16),) * 2
        out_specs = (vmem, hbm)
    return pl.pallas_call(
        lambda *refs: layer_kernel(final, req, *refs),
        name="last_layer" if final else "first_layer",
        out_shape=outs,
        in_specs=specs,
        out_specs=out_specs,
        scratch_shapes=scratch,
        input_output_aliases=aliases,
        compiler_params=pltpu.CompilerParams(vmem_limit_bytes=56 << 20),
    )(*operands)


def on_device(
    hidden,
    text_kv,
    stale_kv,
    modulation,
    score_gain,
    qkv_weight,
    out_weight,
    final_mod,
    final_weight,
    latent,
    step_index,
):
    section = lax.axis_index("section")
    shard = lax.axis_index("shard")
    z_hi, x_at, core = shard // 8, (shard // 2) % 4, shard % 2

    qkv = qkv_weight[0]
    half_kv = qkv[:, HW:]
    half_oq = jnp.concatenate([qkv[:, :HW], out_weight[0].T], 1)
    keep = jnp.where(core == 0, half_kv, half_oq)
    got = core_flip(jnp.where(core == 0, half_oq, half_kv))
    mine_block = jnp.concatenate(
        [jnp.where(core == 0, keep, got), jnp.where(core == 0, got, keep)], 0
    )
    near_z, near_x = mine_block[:, :ZC], mine_block[:, ZC:]
    text = jnp.pad(text_kv[0], ((0, 0), (0, TXT_PAD - TXT), (0, 0)))

    before_x, after_x = x_shift(near_x, 1), x_shift(near_x, -1)
    opposite_z = z_flip(near_z)
    before_y, after_y = y_shift(stale_kv[0], 1), y_shift(stale_kv[0], -1)
    far_x = x_relay(jnp.where(core == 0, after(before_x, text), after_x))
    three_x = jnp.concatenate([near_x, before_x, after_x], 0)
    opposite_three = z_flip(three_x)
    pair_z = jnp.concatenate([near_z, opposite_z], 0)
    before_z, after_z = x_shift(pair_z, 1), x_shift(pair_z, -1)
    far_y = y_relay(jnp.where(core == 0, after(before_y, far_x), after_y))
    far_z = x_relay(jnp.where(core == 0, before_z, after_z))
    opposite_far = z_flip(after(far_x, opposite_three))
    four_x = jnp.concatenate([three_x, far_x], 0)
    their_pair = core_flip(after(pair_z, before_z))
    their_four_x = core_flip(after(four_x, before_z))
    their_before_z = core_flip(after(before_z, far_y))
    their_after_z = core_flip(after(after_z, far_y))
    their_far_z = core_flip(after(far_z, far_y))
    their_opposite_three = core_flip(after(opposite_three, far_y))
    their_opposite_far = core_flip(after(opposite_far, far_y))
    mine = (pair_z, before_z, after_z, far_z, four_x, opposite_three, opposite_far)
    theirs = (their_pair, their_before_z, their_after_z, their_far_z,
              their_four_x, their_opposite_three, their_opposite_far)
    stale = (before_y, after_y, far_y)
    gain = jnp.tile(score_gain[0] * (1.0 / math.sqrt(HEAD)), WIDE // HEAD)[None, :]
    rows = [
        ((z_hi ^ slot) * 4 + (x_at + dx) % 4) * BLK for slot in range(2) for dx in (0, 3, 1, 2)
    ]
    scalars = jnp.stack([core, *rows, section]).astype(jnp.int32)

    def layer(x, r, last=None):
        return run_layer(
            scalars, x, modulation[0], gain, mine, theirs, stale, text, r, last
        )

    fresh_first, arrived = [], []
    for r in range(2):
        x_next, fresh = layer(hidden, r)
        fresh_first.append(fresh)
        arrived.append(lax.ppermute(x_next, "section", [(0, 1)]))
    velocity, new_kv = [], None
    for r in range(2):
        low, new_kv, high = layer(arrived[r], r, (final_mod, final_weight, fresh_first[r], new_kv))
        sent = lax.ppermute(low, "section", [(1, 0)])
        velocity.append(jnp.where(section == 0, sent.astype(jnp.float32), high))
    velocity_mine = jnp.stack(velocity)
    sig = sigma_of(step_index)[:, None, None]
    sig_next = sigma_of(step_index + 1)[:, None, None]
    latent_next = latent + (sig_next - sig) * velocity_mine
    denoised = latent - sig * velocity_mine
    return (new_kv[None], latent_next, denoised)


def solution(mesh):
    in_specs = (
        P("shard", "patch", None),
        P("section", "shard", None, None),
        P("section", "shard", "patch", None),
        P("section", "shard", None, None),
        P("section", None),
        P("section", "shard", None),
        P("section", None, "shard"),
        P("shard", None, None),
        P(),
        P("shard", ("patch", "section"), None),
        P("shard"),
    )
    out_specs = (
        P("section", "shard", "patch", None),
        P("shard", ("patch", "section"), None),
        P("shard", ("patch", "section"), None),
    )
    return jax.shard_map(
        on_device, mesh=mesh, in_specs=in_specs, out_specs=out_specs, check_vma=False
    )
```
